128 devices in a mesh: dp: 4 (over z), expert: 32 (over y, x, core).
Axes of the slice: x: 4, y: 4, z: 4, core: 2. Of those that a mesh axis runs over, the one named last changes fastest.
Arguments:
- tokens: bfloat16 [16384, 2560], P(('dp', 'expert')), may hold values from -6 to 6
- expert_ids: int32 [16384, 6], P(('dp', 'expert')), may hold values from 0 to 31, as said below
- gate_values: float32 [16384, 6], P(('dp', 'expert')), may hold values from 0.05 to 0.5
- w_gate: bfloat16 [32, 2560, 768], P('expert'), may hold values from -0.125 to 0.125
- w_up: bfloat16 [32, 2560, 768], P('expert'), may hold values from -0.125 to 0.125
- w_down: bfloat16 [32, 768, 2560], P('expert'), may hold values from -0.21875 to 0.21875
Outputs:
- moe_out: bfloat16 [16384, 2560], P(('dp', 'expert'))
The draws below stay inside these ranges and needn't reach their ends.
Inputs may be any that keep to these rules, and one draw needn't show every extreme that they name: `expert_ids`: within each block of 128 rows (one device's tokens), column 0 of every row holds one of two experts that are the same for all devices of a dp group, each of them in 56 to 72 rows, and no other entry names them; the two experts of different dp groups are different; the entries of a row differ; any other expert is named by at most 33 rows of one device, and in every dp group one such expert is named by exactly 33 rows of each of its devices; in some dp group other than the first, one of the two is named by 72 rows of every device, and that expert is named by exactly 33 rows of every device of the first dp group.
All inputs are finite; a program needn't handle non-finite values.
Results may differ from the reference program's by a relative error of at most 0.0058.
Values may be sent and summed in bfloat16 or wider, within the bound.
A program may use at most 128 MiB of HBM per device.

```python
import jax
import jax.numpy as jnp
from jax import lax

D = 2560
F = 768
TOPK = 6
TOK_DEV = 128
EXPERTS = 32
ROWS = 16384
HOTMIN = 56
HOTMAX = 72
CAPN = 33
N_DP = 4
N_EXPERT = 32


def draw_expert_ids(key, part):
    others_count = EXPERTS - 2
    picks = 5 * TOK_DEV
    pool_size = others_count * CAPN
    global_order = jax.random.permutation(jax.random.fold_in(key, 5), EXPERTS).astype(jnp.int32)
    full_group = jax.random.randint(jax.random.fold_in(key, 7), (), 1, N_DP)
    target_side = jax.random.randint(jax.random.fold_in(key, 9), (), 0, 2)
    target = global_order[2 * full_group + target_side]

    def group_setup(group_number):
        group_key = jax.random.fold_in(key, 11 + group_number)
        base = jnp.arange(others_count, dtype=jnp.int32)
        mapped = base + 2 * (base >= 2 * group_number).astype(jnp.int32)
        shuffled = jax.random.permutation(group_key, others_count).astype(jnp.int32)
        others = global_order[mapped[shuffled]]
        favoured_pair = jnp.stack([global_order[2 * group_number], global_order[2 * group_number + 1]])
        ranking = jnp.concatenate([favoured_pair, others]).astype(jnp.int32)
        random_forced = jax.random.randint(jax.random.fold_in(group_key, 1), (), 0, others_count)
        target_place = jnp.argmax((others == target).astype(jnp.int32)).astype(jnp.int32)
        forced = jnp.where(group_number == 0, target_place, random_forced).astype(jnp.int32)
        return (ranking, forced)
    rankings, forced_all = jax.vmap(group_setup)(jnp.arange(N_DP, dtype=jnp.int32))

    def block_rows(block_number):
        group_number = block_number // N_EXPERT
        block_key = jax.random.fold_in(key, 1000 + block_number)
        ranking = rankings[group_number]
        forced = forced_all[group_number]
        favoured = jax.random.randint(jax.random.fold_in(block_key, 1), (), HOTMIN, HOTMAX + 1)
        favoured_first = jnp.where(group_number == full_group, jnp.where(target_side == 0, HOTMAX, HOTMIN), favoured)
        pool_ids = jnp.arange(pool_size, dtype=jnp.int32) // CAPN
        random_part = jax.random.randint(jax.random.fold_in(block_key, 2), (pool_size,), 1, 1024)
        scores = jnp.where(pool_ids == forced, 0, random_part) * pool_size + jnp.arange(pool_size, dtype=jnp.int32)
        chosen = jnp.sort(pool_ids[jnp.argsort(scores, stable=True)[:picks]])
        columns = chosen.reshape(5, TOK_DEV).T
        others = ranking[2 + columns]
        favoured_first = jnp.where((group_number == full_group) & (target_side == 1), TOK_DEV - HOTMAX, favoured_first)
        hot_column = jnp.where(jnp.arange(TOK_DEV) < favoured_first, ranking[0], ranking[1])
        rows_block = jnp.concatenate([hot_column[:, None], others], axis=1)
        token_order = jax.random.permutation(jax.random.fold_in(block_key, 3), TOK_DEV)
        return rows_block[token_order]
    every_block = jax.vmap(block_rows)(jnp.arange(N_DP * N_EXPERT, dtype=jnp.int32))
    return every_block.reshape(ROWS, TOPK).astype(jnp.int32)


def steps_of(own_key, shape, shards, smallest, largest):
    def one(axis_at, shards_of):
        steps = jax.random.uniform(jax.random.fold_in(jax.random.fold_in(own_key, 6), axis_at), (shards_of,), jnp.float32, smallest / len(shards), largest / len(shards))
        return jnp.repeat(jnp.exp(steps), shape[axis_at] // shards_of).reshape((-1,) + (1,) * (len(shape) - axis_at - 1))

    factor_of = one(*shards[0])
    for cut in shards[1:]:
        factor_of = factor_of * one(*cut)
    return factor_of


def centred(own_key, shape, spread, reach, pieces=(), held_as=jnp.bfloat16):
    level = steps_of(own_key, shape, pieces, -0.22, 0.18) if pieces else 1.0
    result = jax.random.normal(own_key, shape, jnp.float32) * spread * level
    return jnp.minimum(jnp.maximum(result, -reach), reach).astype(held_as)


def setup_inputs(seed: int = 0) -> dict:
    arg_keys = jax.random.split(jax.random.key(seed), 7)
    tokens = centred(arg_keys[0], (ROWS, D), 1.0, 6.0, ((0, 128),))
    expert_ids = draw_expert_ids(jax.random.fold_in(arg_keys[6], 71), 0)
    gate_values = jnp.clip(0.05 + 0.45 * jax.random.uniform(arg_keys[2], (ROWS, TOPK), jnp.float32) ** steps_of(arg_keys[2], (ROWS, TOPK), ((0, 128),), -0.2, 0.2), 0.05, 0.5)
    w_gate = centred(arg_keys[3], (EXPERTS, D, F), D ** -0.5, 0.125, ((0, 32),))
    w_up = centred(arg_keys[4], (EXPERTS, D, F), D ** -0.5, 0.125, ((0, 32),))
    w_down = centred(arg_keys[5], (EXPERTS, F, D), F ** -0.5, 0.21875, ((0, 32),))
    return {"tokens": tokens, "expert_ids": expert_ids, "gate_values": gate_values, "w_gate": w_gate, "w_up": w_up, "w_down": w_down}


def expert_apply(row_block, gate_matrix, up_matrix, down_matrix):
    gate_part = jnp.dot(row_block, gate_matrix, preferred_element_type=jnp.float32)
    up_part = jnp.dot(row_block, up_matrix, preferred_element_type=jnp.float32)
    hidden = (jax.nn.silu(gate_part) * up_part).astype(jnp.bfloat16)
    return jnp.dot(hidden, down_matrix, preferred_element_type=jnp.float32).astype(jnp.bfloat16)


def reference(tokens, expert_ids, gate_values, w_gate, w_up, w_down):
    flat_ids = expert_ids.reshape(-1).astype(jnp.int32)
    pair_count = flat_ids.shape[0]
    block_size = 256
    counts = jnp.zeros((EXPERTS,), jnp.int32).at[flat_ids].add(1)
    padded_counts = (counts + block_size - 1) // block_size * block_size
    starts = jnp.cumsum(counts) - counts
    padded_starts = jnp.cumsum(padded_counts) - padded_counts
    sorted_pairs = jnp.argsort(flat_ids, stable=True).astype(jnp.int32)
    flat_gates = gate_values.reshape(-1)
    block_total = (pair_count + block_size - 1) // block_size + EXPERTS

    def add_block(summed, block_number):
        block_start = block_number * block_size
        expert = (jnp.sum((padded_starts <= block_start).astype(jnp.int32)) - 1).astype(jnp.int32)
        within = block_start - padded_starts[expert] + jnp.arange(block_size, dtype=jnp.int32)
        in_range = within < counts[expert]
        pair_index = sorted_pairs[jnp.clip(starts[expert] + within, 0, pair_count - 1)]
        token_index = pair_index // TOPK
        outputs = expert_apply(tokens[token_index], w_gate[expert], w_up[expert], w_down[expert])
        weights = jnp.where(in_range, flat_gates[pair_index], jnp.zeros((), flat_gates.dtype))
        summed = summed.at[token_index].add(weights[:, None] * outputs.astype(summed.dtype))
        return summed, None

    summed, unused = lax.scan(add_block, jnp.zeros((ROWS, D), jnp.float32), jnp.arange(block_total, dtype=jnp.int32))
    return summed.astype(jnp.bfloat16)
```

```python
import jax
import jax.numpy as jnp
from jax import lax
from jax.sharding import PartitionSpec as P


def expert_apply(row_block, gate_matrix, up_matrix, down_matrix):
    gate_part = jnp.dot(row_block, gate_matrix, preferred_element_type=jnp.float32)
    up_part = jnp.dot(row_block, up_matrix, preferred_element_type=jnp.float32)
    hidden = (jax.nn.silu(gate_part) * up_part).astype(jnp.bfloat16)
    return jnp.dot(hidden, down_matrix, preferred_element_type=jnp.float32).astype(jnp.bfloat16)


def split_bf16(values):
    first = values.astype(jnp.bfloat16)
    rest = values - first.astype(jnp.float32)
    second = rest.astype(jnp.bfloat16)
    third = (rest - second.astype(jnp.float32)).astype(jnp.bfloat16)
    return first, second, third


def shards(tokens, expert_ids, gate_values, w_gate, w_up, w_down):
    token_count, features = tokens.shape
    topk_width = expert_ids.shape[1]
    local_count = w_gate.shape[0]
    experts_all = lax.axis_size("expert") * local_count
    other_bound = min(
        token_count,
        ((topk_width - 1) * token_count + experts_all - 3) // (experts_all - 2) * 3 // 2,
    )
    favoured_bound = token_count * 9 // 16
    slot_bound = max(favoured_bound, other_bound)
    buffer_rows = experts_all * slot_bound

    flat_ids = expert_ids.reshape(-1)
    one_hot = (flat_ids[:, None] == jnp.arange(experts_all, dtype=jnp.int32)[None, :]).astype(
        jnp.int32
    )
    earlier = jnp.cumsum(one_hot, axis=0) - one_hot
    slot_of = jnp.sum(earlier * one_hot, axis=1)
    places = (flat_ids * slot_bound + slot_of).reshape(token_count, topk_width)

    hit = places[:, :, None] == jnp.arange(buffer_rows, dtype=jnp.int32)[None, None, :]
    pick = jnp.any(hit, axis=1).astype(jnp.bfloat16)
    outgoing = jnp.einsum(
        "tr,td->rd", pick, tokens, preferred_element_type=jnp.float32
    ).astype(jnp.bfloat16)

    received = lax.all_to_all(
        outgoing.reshape(experts_all, slot_bound, features),
        "expert",
        split_axis=0,
        concat_axis=0,
        tiled=True,
    )
    answered = expert_apply(
        received.reshape(buffer_rows, features), w_gate[0], w_up[0], w_down[0]
    )
    returned = lax.all_to_all(
        answered.reshape(experts_all, slot_bound, features),
        "expert",
        split_axis=0,
        concat_axis=0,
        tiled=True,
    ).reshape(buffer_rows, features)

    weights = jnp.sum(jnp.where(hit, gate_values[:, :, None], 0.0), axis=1)
    summed = None
    for part in split_bf16(weights):
        term = jnp.dot(part, returned, preferred_element_type=jnp.float32)
        summed = term if summed is None else summed + term
    return summed.astype(jnp.bfloat16)


def solution(mesh):
    placed = (
        P(("dp", "expert"), None),
        P(("dp", "expert"), None),
        P(("dp", "expert"), None),
        P("expert", None, None),
        P("expert", None, None),
        P("expert", None, None),
    )
    return jax.shard_map(
        shards, mesh=mesh, in_specs=placed, out_specs=P(("dp", "expert"), None), check_vma=False
    )
```

```python
import jax
import jax.numpy as jnp
from jax import lax
from jax.sharding import PartitionSpec as P


def expert_apply(row_block, gate_matrix, up_matrix, down_matrix):
    gate_part = jnp.dot(row_block, gate_matrix, preferred_element_type=jnp.float32)
    up_part = jnp.dot(row_block, up_matrix, preferred_element_type=jnp.float32)
    hidden = (jax.nn.silu(gate_part) * up_part).astype(jnp.bfloat16)
    return jnp.dot(hidden, down_matrix, preferred_element_type=jnp.float32).astype(jnp.bfloat16)


def split_bf16(values):
    first = values.astype(jnp.bfloat16)
    rest = values - first.astype(jnp.float32)
    second = rest.astype(jnp.bfloat16)
    third = (rest - second.astype(jnp.float32)).astype(jnp.bfloat16)
    return first, second, third


def shards(tokens, expert_ids, gate_values, w_gate, w_up, w_down):
    token_count, features = tokens.shape
    topk_width = expert_ids.shape[1]
    local_count = w_gate.shape[0]
    experts_all = lax.axis_size("expert") * local_count
    other_bound = min(
        token_count,
        ((topk_width - 1) * token_count + experts_all - 3) // (experts_all - 2) * 3 // 2,
    )
    favoured_bound = token_count * 9 // 16
    slot_bound = max(favoured_bound, other_bound)
    buffer_rows = experts_all * slot_bound

    flat_ids = expert_ids.reshape(-1)
    one_hot = (flat_ids[:, None] == jnp.arange(experts_all, dtype=jnp.int32)[None, :]).astype(
        jnp.int32
    )
    earlier = jnp.cumsum(one_hot, axis=0) - one_hot
    slot_of = jnp.sum(earlier * one_hot, axis=1)
    places = (flat_ids * slot_bound + slot_of).reshape(token_count, topk_width)

    hit = places[:, :, None] == jnp.arange(buffer_rows, dtype=jnp.int32)[None, None, :]
    pick = jnp.any(hit, axis=1).astype(jnp.bfloat16)
    outgoing = jnp.einsum(
        "tr,td->rd", pick, tokens, preferred_element_type=jnp.float32
    ).astype(jnp.bfloat16)

    chunks = 2
    chunk_slots = slot_bound // chunks
    staged = outgoing.reshape(experts_all, slot_bound, features)
    answers = []
    for chunk in range(chunks):
        received = lax.all_to_all(
            staged[:, chunk * chunk_slots:(chunk + 1) * chunk_slots],
            "expert",
            split_axis=0,
            concat_axis=0,
            tiled=True,
        )
        answered = expert_apply(
            received.reshape(-1, features), w_gate[0], w_up[0], w_down[0]
        )
        answers.append(
            lax.all_to_all(
                answered.reshape(experts_all, chunk_slots, features),
                "expert",
                split_axis=0,
                concat_axis=0,
                tiled=True,
            )
        )
    returned = jnp.concatenate(answers, axis=1).reshape(buffer_rows, features)

    weights = jnp.sum(jnp.where(hit, gate_values[:, :, None], 0.0), axis=1)
    stacked = jnp.concatenate(split_bf16(weights), axis=0)
    terms = jnp.dot(stacked, returned, preferred_element_type=jnp.float32)
    summed = jnp.sum(terms.reshape(3, token_count, features), axis=0)
    return summed.astype(jnp.bfloat16)


def solution(mesh):
    placed = (
        P(("dp", "expert"), None),
        P(("dp", "expert"), None),
        P(("dp", "expert"), None),
        P("expert", None, None),
        P("expert", None, None),
        P("expert", None, None),
    )
    return jax.shard_map(
        shards, mesh=mesh, in_specs=placed, out_specs=P(("dp", "expert"), None), check_vma=False
    )
```

```python
import functools

import jax
import jax.numpy as jnp
from jax import lax
from jax.experimental import pallas as pl
from jax.experimental.pallas import tpu as pltpu
from jax.sharding import PartitionSpec as P

MESH = pl.DeviceIdType.MESH


def exchange_kernel(n, x_ref, y_ref, send_sem, recv_sem, local_sem):
    me = lax.axis_index("expert")
    barrier = pltpu.get_barrier_semaphore()

    def greet(k, carry):
        pl.semaphore_signal(
            barrier, inc=1, device_id={"expert": lax.rem(me + k, n)}, device_id_type=MESH
        )
        return carry

    lax.fori_loop(1, n, greet, 0)
    pl.semaphore_wait(barrier, n - 1)
    local = pltpu.make_async_copy(x_ref.at[me], y_ref.at[me], local_sem)
    local.start()

    def remote(k):
        target = lax.rem(me + k, n)
        return pltpu.make_async_remote_copy(
            src_ref=x_ref.at[target],
            dst_ref=y_ref.at[me],
            send_sem=send_sem.at[k],
            recv_sem=recv_sem.at[k],
            device_id={"expert": target},
            device_id_type=MESH,
        )

    def start(k, carry):
        remote(k).start()
        return carry

    def finish(k, carry):
        remote(k).wait()
        return carry

    lax.fori_loop(1, n, start, 0)
    lax.fori_loop(1, n, finish, 0)
    local.wait()


def exchange(blocks, collective_id):
    n = lax.axis_size("expert")
    return pl.pallas_call(
        functools.partial(exchange_kernel, n),
        out_shape=jax.ShapeDtypeStruct(blocks.shape, blocks.dtype),
        in_specs=[pl.BlockSpec(memory_space=pl.ANY)],
        out_specs=pl.BlockSpec(memory_space=pl.ANY),
        scratch_shapes=[
            pltpu.SemaphoreType.DMA((n,)),
            pltpu.SemaphoreType.DMA((n,)),
            pltpu.SemaphoreType.DMA,
        ],
        compiler_params=pltpu.CompilerParams(collective_id=collective_id, has_side_effects=True),
    )(blocks)


def expert_apply(row_block, gate_matrix, up_matrix, down_matrix):
    gate_part = jnp.dot(row_block, gate_matrix, preferred_element_type=jnp.float32)
    up_part = jnp.dot(row_block, up_matrix, preferred_element_type=jnp.float32)
    hidden = (jax.nn.silu(gate_part) * up_part).astype(jnp.bfloat16)
    return jnp.dot(hidden, down_matrix, preferred_element_type=jnp.float32).astype(jnp.bfloat16)


def split_bf16(values):
    first = lax.reduce_precision(values, exponent_bits=8, mantissa_bits=7)
    rest = values - first
    second = lax.reduce_precision(rest, exponent_bits=8, mantissa_bits=7)
    third = rest - second
    return tuple(part.astype(jnp.bfloat16) for part in (first, second, third))


def shards(tokens, expert_ids, gate_values, w_gate, w_up, w_down):
    token_count, features = tokens.shape
    topk_width = expert_ids.shape[1]
    local_count = w_gate.shape[0]
    experts_all = lax.axis_size("expert") * local_count
    other_bound = min(
        token_count,
        ((topk_width - 1) * token_count + experts_all - 3) // (experts_all - 2) * 3 // 2,
    )
    favoured_bound = token_count * 9 // 16
    slot_bound = max(favoured_bound, other_bound)
    buffer_rows = experts_all * slot_bound

    flat_ids = expert_ids.reshape(-1)
    one_hot = (flat_ids[:, None] == jnp.arange(experts_all, dtype=jnp.int32)[None, :]).astype(
        jnp.int32
    )
    earlier = jnp.cumsum(one_hot, axis=0) - one_hot
    slot_of = jnp.sum(earlier * one_hot, axis=1)
    places = (flat_ids * slot_bound + slot_of).reshape(token_count, topk_width)

    hit = places[:, :, None] == jnp.arange(buffer_rows, dtype=jnp.int32)[None, None, :]
    pick = jnp.any(hit, axis=1).astype(jnp.bfloat16)
    outgoing = jnp.einsum(
        "tr,td->rd", pick, tokens, preferred_element_type=jnp.float32
    ).astype(jnp.bfloat16)

    received = exchange(outgoing.reshape(experts_all, slot_bound, features), 0)
    answered = expert_apply(
        received.reshape(buffer_rows, features), w_gate[0], w_up[0], w_down[0]
    )
    returned = exchange(answered.reshape(experts_all, slot_bound, features), 1).reshape(
        buffer_rows, features
    )

    weights = jnp.sum(jnp.where(hit, gate_values[:, :, None], 0.0), axis=1)
    stacked = jnp.concatenate(split_bf16(weights), axis=0)
    terms = jnp.dot(stacked, returned, preferred_element_type=jnp.float32)
    summed = jnp.sum(terms.reshape(3, token_count, features), axis=0)
    return summed.astype(jnp.bfloat16)


def solution(mesh):
    placed = (
        P(("dp", "expert"), None),
        P(("dp", "expert"), None),
        P(("dp", "expert"), None),
        P("expert", None, None),
        P("expert", None, None),
        P("expert", None, None),
    )
    return jax.shard_map(
        shards, mesh=mesh, in_specs=placed, out_specs=P(("dp", "expert"), None), check_vma=False
    )
```

```python
import functools

import jax
import jax.numpy as jnp
from jax import lax
from jax.experimental import pallas as pl
from jax.experimental.pallas import tpu as pltpu
from jax.sharding import PartitionSpec as P

MESH = pl.DeviceIdType.MESH


def exchange_kernel(n, x_ref, y_ref, send_sem, recv_sem, local_sem):
    me = lax.axis_index("expert")
    barrier = pltpu.get_barrier_semaphore()

    def greet(k, carry):
        pl.semaphore_signal(
            barrier, inc=1, device_id={"expert": lax.rem(me + k, n)}, device_id_type=MESH
        )
        return carry

    lax.fori_loop(1, n, greet, 0)
    pl.semaphore_wait(barrier, n - 1)
    local = pltpu.make_async_copy(x_ref.at[me], y_ref.at[me], local_sem)
    local.start()

    def remote(k):
        target = lax.rem(me + k, n)
        return pltpu.make_async_remote_copy(
            src_ref=x_ref.at[target],
            dst_ref=y_ref.at[me],
            send_sem=send_sem.at[k],
            recv_sem=recv_sem.at[k],
            device_id={"expert": target},
            device_id_type=MESH,
        )

    def start(k, carry):
        remote(k).start()
        return carry

    def finish(k, carry):
        remote(k).wait()
        return carry

    lax.fori_loop(1, n, start, 0)
    lax.fori_loop(1, n, finish, 0)
    local.wait()


def exchange(blocks, collective_id):
    n = lax.axis_size("expert")
    return pl.pallas_call(
        functools.partial(exchange_kernel, n),
        out_shape=jax.ShapeDtypeStruct(blocks.shape, blocks.dtype),
        in_specs=[pl.BlockSpec(memory_space=pl.ANY)],
        out_specs=pl.BlockSpec(memory_space=pl.ANY),
        scratch_shapes=[
            pltpu.SemaphoreType.DMA((n,)),
            pltpu.SemaphoreType.DMA((n,)),
            pltpu.SemaphoreType.DMA,
        ],
        compiler_params=pltpu.CompilerParams(collective_id=collective_id, has_side_effects=True),
    )(blocks)


def expert_apply(row_block, gate_matrix, up_matrix, down_matrix):
    gate_part = jnp.dot(row_block, gate_matrix, preferred_element_type=jnp.float32)
    up_part = jnp.dot(row_block, up_matrix, preferred_element_type=jnp.float32)
    hidden = (jax.nn.silu(gate_part) * up_part).astype(jnp.bfloat16)
    return jnp.dot(hidden, down_matrix, preferred_element_type=jnp.float32).astype(jnp.bfloat16)


def split_bf16(values):
    first = lax.reduce_precision(values, exponent_bits=8, mantissa_bits=7)
    rest = values - first
    second = lax.reduce_precision(rest, exponent_bits=8, mantissa_bits=7)
    third = rest - second
    return tuple(part.astype(jnp.bfloat16) for part in (first, second, third))


def shards(tokens, expert_ids, gate_values, w_gate, w_up, w_down):
    token_count, features = tokens.shape
    topk_width = expert_ids.shape[1]
    local_count = w_gate.shape[0]
    experts_all = lax.axis_size("expert") * local_count
    other_bound = min(
        token_count,
        ((topk_width - 1) * token_count + experts_all - 3) // (experts_all - 2) * 3 // 2,
    )
    favoured_bound = token_count * 9 // 16
    slot_bound = max(favoured_bound, other_bound)
    buffer_rows = experts_all * slot_bound

    flat_ids = expert_ids.reshape(-1)
    one_hot = (flat_ids[:, None] == jnp.arange(experts_all, dtype=jnp.int32)[None, :]).astype(
        jnp.int32
    )
    earlier = jnp.cumsum(one_hot, axis=0) - one_hot
    slot_of = jnp.sum(earlier * one_hot, axis=1)
    places = (flat_ids * slot_bound + slot_of).reshape(token_count, topk_width)

    chunk_sizes = (slot_bound // 2, slot_bound - slot_bound // 2)
    weight_parts = split_bf16(gate_values)
    summed = None
    begin = 0
    for size in chunk_sizes:
        inside = (slot_of >= begin) & (slot_of < begin + size)
        local_place = jnp.where(inside, flat_ids * size + slot_of - begin, -1)
        hit = (
            local_place.reshape(token_count, topk_width)[:, :, None]
            == jnp.arange(experts_all * size, dtype=jnp.int32)[None, None, :]
        ).reshape(token_count, topk_width, experts_all, size)
        begin += size
        pick = jnp.any(hit, axis=1).astype(jnp.bfloat16)
        outgoing = jnp.einsum(
            "tes,td->esd", pick, tokens, preferred_element_type=jnp.float32
        ).astype(jnp.bfloat16)
        received = lax.all_to_all(outgoing, "expert", split_axis=0, concat_axis=0, tiled=True)
        answered = expert_apply(received, w_gate[0], w_up[0], w_down[0])
        returned = lax.all_to_all(answered, "expert", split_axis=0, concat_axis=0, tiled=True)
        stacked = jnp.stack(
            [
                jnp.sum(jnp.where(hit, part.astype(jnp.float32)[:, :, None, None], 0.0), axis=1)
                for part in weight_parts
            ]
        ).astype(jnp.bfloat16)
        terms = jnp.einsum("ptes,esd->ptd", stacked, returned, preferred_element_type=jnp.float32)
        term = jnp.sum(terms, axis=0)
        summed = term if summed is None else summed + term
    return summed.astype(jnp.bfloat16)


def solution(mesh):
    placed = (
        P(("dp", "expert"), None),
        P(("dp", "expert"), None),
        P(("dp", "expert"), None),
        P("expert", None, None),
        P("expert", None, None),
        P("expert", None, None),
    )
    return jax.shard_map(
        shards, mesh=mesh, in_specs=placed, out_specs=P(("dp", "expert"), None), check_vma=False
    )
```

```python
import functools

import jax
import jax.numpy as jnp
from jax import lax
from jax.experimental import pallas as pl
from jax.experimental.pallas import tpu as pltpu
from jax.sharding import PartitionSpec as P

MESH = pl.DeviceIdType.MESH


def exchange_kernel(n, x_ref, y_ref, send_sem, recv_sem, local_sem):
    me = lax.axis_index("expert")
    barrier = pltpu.get_barrier_semaphore()

    def greet(k, carry):
        pl.semaphore_signal(
            barrier, inc=1, device_id={"expert": lax.rem(me + k, n)}, device_id_type=MESH
        )
        return carry

    lax.fori_loop(1, n, greet, 0)
    pl.semaphore_wait(barrier, n - 1)
    local = pltpu.make_async_copy(x_ref.at[me], y_ref.at[me], local_sem)
    local.start()

    def remote(k):
        target = lax.rem(me + k, n)
        return pltpu.make_async_remote_copy(
            src_ref=x_ref.at[target],
            dst_ref=y_ref.at[me],
            send_sem=send_sem.at[k],
            recv_sem=recv_sem.at[k],
            device_id={"expert": target},
            device_id_type=MESH,
        )

    def start(k, carry):
        remote(k).start()
        return carry

    def finish(k, carry):
        remote(k).wait()
        return carry

    lax.fori_loop(1, n, start, 0)
    lax.fori_loop(1, n, finish, 0)
    local.wait()


def exchange(blocks, collective_id):
    n = lax.axis_size("expert")
    return pl.pallas_call(
        functools.partial(exchange_kernel, n),
        out_shape=jax.ShapeDtypeStruct(blocks.shape, blocks.dtype),
        in_specs=[pl.BlockSpec(memory_space=pl.ANY)],
        out_specs=pl.BlockSpec(memory_space=pl.ANY),
        scratch_shapes=[
            pltpu.SemaphoreType.DMA((n,)),
            pltpu.SemaphoreType.DMA((n,)),
            pltpu.SemaphoreType.DMA,
        ],
        compiler_params=pltpu.CompilerParams(collective_id=collective_id, has_side_effects=True),
    )(blocks)


def expert_apply(row_block, gate_matrix, up_matrix, down_matrix):
    gate_part = jnp.dot(row_block, gate_matrix, preferred_element_type=jnp.float32)
    up_part = jnp.dot(row_block, up_matrix, preferred_element_type=jnp.float32)
    hidden = (jax.nn.silu(gate_part) * up_part).astype(jnp.bfloat16)
    return jnp.dot(hidden, down_matrix, preferred_element_type=jnp.float32).astype(jnp.bfloat16)


def split_bf16(values):
    first = lax.reduce_precision(values, exponent_bits=8, mantissa_bits=7)
    rest = values - first
    second = lax.reduce_precision(rest, exponent_bits=8, mantissa_bits=7)
    third = rest - second
    return tuple(part.astype(jnp.bfloat16) for part in (first, second, third))


def shards(tokens, expert_ids, gate_values, w_gate, w_up, w_down):
    token_count, features = tokens.shape
    topk_width = expert_ids.shape[1]
    local_count = w_gate.shape[0]
    experts_all = lax.axis_size("expert") * local_count
    other_bound = min(
        token_count,
        ((topk_width - 1) * token_count + experts_all - 3) // (experts_all - 2) * 3 // 2,
    )
    favoured_bound = token_count * 9 // 16
    slot_bound = max(favoured_bound, other_bound)
    buffer_rows = experts_all * slot_bound

    flat_ids = expert_ids.reshape(-1)
    one_hot = (flat_ids[:, None] == jnp.arange(experts_all, dtype=jnp.int32)[None, :]).astype(
        jnp.int32
    )
    earlier = jnp.cumsum(one_hot, axis=0) - one_hot
    slot_of = jnp.sum(earlier * one_hot, axis=1)
    places = (flat_ids * slot_bound + slot_of).reshape(token_count, topk_width)

    hit = (
        places[:, :, None] == jnp.arange(buffer_rows, dtype=jnp.int32)[None, None, :]
    ).reshape(token_count, topk_width, experts_all, slot_bound)
    pick = jnp.any(hit, axis=1).astype(jnp.bfloat16)
    outgoing = jnp.einsum(
        "tes,td->esd", pick, tokens, preferred_element_type=jnp.float32
    ).astype(jnp.bfloat16)
    received = lax.all_to_all(outgoing, "expert", split_axis=0, concat_axis=0, tiled=True)

    small = slot_bound // 9
    weight_parts = split_bf16(gate_values)
    summed = None
    for begin, end in ((0, small), (small, slot_bound)):
        answered = expert_apply(received[:, begin:end], w_gate[0], w_up[0], w_down[0])
        returned = lax.all_to_all(answered, "expert", split_axis=0, concat_axis=0, tiled=True)
        stacked = jnp.stack(
            [
                jnp.sum(
                    jnp.where(
                        hit[:, :, :, begin:end], part.astype(jnp.float32)[:, :, None, None], 0.0
                    ),
                    axis=1,
                )
                for part in weight_parts
            ]
        ).astype(jnp.bfloat16)
        terms = jnp.einsum("ptes,esd->ptd", stacked, returned, preferred_element_type=jnp.float32)
        term = jnp.sum(terms, axis=0)
        summed = term if summed is None else summed + term
    return summed.astype(jnp.bfloat16)


def solution(mesh):
    placed = (
        P(("dp", "expert"), None),
        P(("dp", "expert"), None),
        P(("dp", "expert"), None),
        P("expert", None, None),
        P("expert", None, None),
        P("expert", None, None),
    )
    return jax.shard_map(
        shards, mesh=mesh, in_specs=placed, out_specs=P(("dp", "expert"), None), check_vma=False
    )
```

```python
import functools

import jax
import jax.numpy as jnp
from jax import lax
from jax.experimental import pallas as pl
from jax.experimental.pallas import tpu as pltpu
from jax.sharding import PartitionSpec as P

MESH = pl.DeviceIdType.MESH


def exchange_kernel(n, x_ref, y_ref, send_sem, recv_sem, local_sem):
    me = lax.axis_index("expert")
    barrier = pltpu.get_barrier_semaphore()

    def greet(k, carry):
        pl.semaphore_signal(
            barrier, inc=1, device_id={"expert": lax.rem(me + k, n)}, device_id_type=MESH
        )
        return carry

    lax.fori_loop(1, n, greet, 0)
    pl.semaphore_wait(barrier, n - 1)
    local = pltpu.make_async_copy(x_ref.at[me], y_ref.at[me], local_sem)
    local.start()

    def remote(k):
        target = lax.rem(me + k, n)
        return pltpu.make_async_remote_copy(
            src_ref=x_ref.at[target],
            dst_ref=y_ref.at[me],
            send_sem=send_sem.at[k],
            recv_sem=recv_sem.at[k],
            device_id={"expert": target},
            device_id_type=MESH,
        )

    def start(k, carry):
        remote(k).start()
        return carry

    def finish(k, carry):
        remote(k).wait()
        return carry

    lax.fori_loop(1, n, start, 0)
    lax.fori_loop(1, n, finish, 0)
    local.wait()


def exchange(blocks, collective_id):
    n = lax.axis_size("expert")
    return pl.pallas_call(
        functools.partial(exchange_kernel, n),
        out_shape=jax.ShapeDtypeStruct(blocks.shape, blocks.dtype),
        in_specs=[pl.BlockSpec(memory_space=pl.ANY)],
        out_specs=pl.BlockSpec(memory_space=pl.ANY),
        scratch_shapes=[
            pltpu.SemaphoreType.DMA((n,)),
            pltpu.SemaphoreType.DMA((n,)),
            pltpu.SemaphoreType.DMA,
        ],
        compiler_params=pltpu.CompilerParams(collective_id=collective_id, has_side_effects=True),
    )(blocks)


def expert_apply(row_block, gate_matrix, up_matrix, down_matrix):
    gate_part = jnp.dot(row_block, gate_matrix, preferred_element_type=jnp.float32)
    up_part = jnp.dot(row_block, up_matrix, preferred_element_type=jnp.float32)
    hidden = (jax.nn.silu(gate_part) * up_part).astype(jnp.bfloat16)
    return jnp.dot(hidden, down_matrix, preferred_element_type=jnp.float32).astype(jnp.bfloat16)


def ffn_kernel(x_ref, gate_ref, up_ref, down_ref, out_ref):
    sources, slots, features = x_ref.shape
    rows = x_ref[...].reshape(sources * slots, features)
    out_ref[...] = expert_apply(rows, gate_ref[...], up_ref[...], down_ref[...]).reshape(
        sources, slots, features
    )


def expert_blocks(received, gate_matrix, up_matrix, down_matrix, slots, per_step):
    sources, _, features = received.shape
    hidden = gate_matrix.shape[1]
    return pl.pallas_call(
        ffn_kernel,
        out_shape=jax.ShapeDtypeStruct((sources, slots, features), received.dtype),
        grid=(sources // per_step,),
        in_specs=[
            pl.BlockSpec((per_step, slots, features), lambda i: (i, 0, 0)),
            pl.BlockSpec((features, hidden), lambda i: (0, 0)),
            pl.BlockSpec((features, hidden), lambda i: (0, 0)),
            pl.BlockSpec((hidden, features), lambda i: (0, 0)),
        ],
        out_specs=pl.BlockSpec((per_step, slots, features), lambda i: (i, 0, 0)),
        compiler_params=pltpu.CompilerParams(vmem_limit_bytes=60 * 1024 * 1024),
        cost_estimate=pl.CostEstimate(
            flops=6 * sources * slots * features * hidden,
            transcendentals=sources * slots * hidden,
            bytes_accessed=2 * (2 * sources * slots * features + 3 * features * hidden),
        ),
    )(received, gate_matrix, up_matrix, down_matrix)


def split_bf16(values):
    first = lax.reduce_precision(values, exponent_bits=8, mantissa_bits=7)
    rest = values - first
    second = lax.reduce_precision(rest, exponent_bits=8, mantissa_bits=7)
    third = rest - second
    return tuple(part.astype(jnp.bfloat16) for part in (first, second, third))


def shards(tokens, expert_ids, gate_values, w_gate, w_up, w_down):
    token_count, features = tokens.shape
    topk_width = expert_ids.shape[1]
    local_count = w_gate.shape[0]
    experts_all = lax.axis_size("expert") * local_count
    other_bound = min(
        token_count,
        ((topk_width - 1) * token_count + experts_all - 3) // (experts_all - 2) * 3 // 2,
    )
    favoured_bound = token_count * 9 // 16
    slot_bound = max(favoured_bound, other_bound)
    buffer_rows = experts_all * slot_bound

    flat_ids = expert_ids.reshape(-1)
    one_hot = (flat_ids[:, None] == jnp.arange(experts_all, dtype=jnp.int32)[None, :]).astype(
        jnp.int32
    )
    earlier = jnp.cumsum(one_hot, axis=0) - one_hot
    slot_of = jnp.sum(earlier * one_hot, axis=1)
    places = (flat_ids * slot_bound + slot_of).reshape(token_count, topk_width)

    hit = (
        places[:, :, None] == jnp.arange(buffer_rows, dtype=jnp.int32)[None, None, :]
    ).reshape(token_count, topk_width, experts_all, slot_bound)
    pick = jnp.any(hit, axis=1).astype(jnp.bfloat16)
    outgoing = jnp.einsum(
        "tes,td->esd", pick, tokens, preferred_element_type=jnp.float32
    ).astype(jnp.bfloat16)
    received = lax.all_to_all(outgoing, "expert", split_axis=0, concat_axis=0, tiled=True)

    large = slot_bound - slot_bound // 9
    weight_parts = split_bf16(gate_values)
    summed = None
    for begin, end in ((large, slot_bound), (0, large)):
        if begin == 0:
            answered = expert_blocks(received, w_gate[0], w_up[0], w_down[0], end, 4)
        else:
            answered = expert_apply(received[:, begin:end], w_gate[0], w_up[0], w_down[0])
        returned = lax.all_to_all(answered, "expert", split_axis=0, concat_axis=0, tiled=True)
        stacked = jnp.stack(
            [
                jnp.sum(
                    jnp.where(
                        hit[:, :, :, begin:end], part.astype(jnp.float32)[:, :, None, None], 0.0
                    ),
                    axis=1,
                )
                for part in weight_parts
            ]
        ).astype(jnp.bfloat16)
        terms = jnp.einsum("ptes,esd->ptd", stacked, returned, preferred_element_type=jnp.float32)
        term = jnp.sum(terms, axis=0)
        summed = term if summed is None else summed + term
    return summed.astype(jnp.bfloat16)


def solution(mesh):
    placed = (
        P(("dp", "expert"), None),
        P(("dp", "expert"), None),
        P(("dp", "expert"), None),
        P("expert", None, None),
        P("expert", None, None),
        P("expert", None, None),
    )
    return jax.shard_map(
        shards, mesh=mesh, in_specs=placed, out_specs=P(("dp", "expert"), None), check_vma=False
    )
```

```python
import functools

import jax
import jax.numpy as jnp
from jax import lax
from jax.experimental import pallas as pl
from jax.experimental.pallas import tpu as pltpu
from jax.sharding import PartitionSpec as P

MESH = pl.DeviceIdType.MESH


def exchange_kernel(n, x_ref, y_ref, send_sem, recv_sem, local_sem):
    me = lax.axis_index("expert")
    barrier = pltpu.get_barrier_semaphore()

    def greet(k, carry):
        pl.semaphore_signal(
            barrier, inc=1, device_id={"expert": lax.rem(me + k, n)}, device_id_type=MESH
        )
        return carry

    lax.fori_loop(1, n, greet, 0)
    pl.semaphore_wait(barrier, n - 1)
    local = pltpu.make_async_copy(x_ref.at[me], y_ref.at[me], local_sem)
    local.start()

    def remote(k):
        target = lax.rem(me + k, n)
        return pltpu.make_async_remote_copy(
            src_ref=x_ref.at[target],
            dst_ref=y_ref.at[me],
            send_sem=send_sem.at[k],
            recv_sem=recv_sem.at[k],
            device_id={"expert": target},
            device_id_type=MESH,
        )

    def start(k, carry):
        remote(k).start()
        return carry

    def finish(k, carry):
        remote(k).wait()
        return carry

    lax.fori_loop(1, n, start, 0)
    lax.fori_loop(1, n, finish, 0)
    local.wait()


def exchange(blocks, collective_id):
    n = lax.axis_size("expert")
    return pl.pallas_call(
        functools.partial(exchange_kernel, n),
        out_shape=jax.ShapeDtypeStruct(blocks.shape, blocks.dtype),
        in_specs=[pl.BlockSpec(memory_space=pl.ANY)],
        out_specs=pl.BlockSpec(memory_space=pl.ANY),
        scratch_shapes=[
            pltpu.SemaphoreType.DMA((n,)),
            pltpu.SemaphoreType.DMA((n,)),
            pltpu.SemaphoreType.DMA,
        ],
        compiler_params=pltpu.CompilerParams(collective_id=collective_id, has_side_effects=True),
    )(blocks)


def expert_apply(row_block, gate_matrix, up_matrix, down_matrix):
    gate_part = jnp.dot(row_block, gate_matrix, preferred_element_type=jnp.float32)
    up_part = jnp.dot(row_block, up_matrix, preferred_element_type=jnp.float32)
    hidden = (jax.nn.silu(gate_part) * up_part).astype(jnp.bfloat16)
    return jnp.dot(hidden, down_matrix, preferred_element_type=jnp.float32).astype(jnp.bfloat16)


def ffn_kernel(x_ref, gate_ref, up_ref, down_ref, *refs):
    out_ref = refs[-1]
    sources, slots, features = x_ref.shape
    rows = x_ref[...].reshape(sources * slots, features)
    out_ref[...] = expert_apply(rows, gate_ref[...], up_ref[...], down_ref[...]).reshape(
        sources, slots, features
    )


def expert_blocks(received, gate_matrix, up_matrix, down_matrix, per_step, into, slot_block):
    sources, slots, features = received.shape
    hidden = gate_matrix.shape[1]
    return pl.pallas_call(
        ffn_kernel,
        out_shape=jax.ShapeDtypeStruct(into.shape, into.dtype),
        grid=(sources // per_step,),
        in_specs=[
            pl.BlockSpec((per_step, slots, features), lambda i: (i, 0, 0)),
            pl.BlockSpec((features, hidden), lambda i: (0, 0)),
            pl.BlockSpec((features, hidden), lambda i: (0, 0)),
            pl.BlockSpec((hidden, features), lambda i: (0, 0)),
            pl.BlockSpec(memory_space=pl.ANY),
        ],
        out_specs=pl.BlockSpec((per_step, slots, features), lambda i: (i, slot_block, 0)),
        input_output_aliases={4: 0},
        compiler_params=pltpu.CompilerParams(vmem_limit_bytes=60 * 1024 * 1024),
        cost_estimate=pl.CostEstimate(
            flops=6 * sources * slots * features * hidden,
            transcendentals=sources * slots * hidden,
            bytes_accessed=2 * (2 * sources * slots * features + 3 * features * hidden),
        ),
    )(received, gate_matrix, up_matrix, down_matrix, into)


def split_bf16(values):
    first = lax.reduce_precision(values, exponent_bits=8, mantissa_bits=7)
    rest = values - first
    second = lax.reduce_precision(rest, exponent_bits=8, mantissa_bits=7)
    third = rest - second
    return tuple(part.astype(jnp.bfloat16) for part in (first, second, third))


def shards(tokens, expert_ids, gate_values, w_gate, w_up, w_down):
    token_count, features = tokens.shape
    topk_width = expert_ids.shape[1]
    local_count = w_gate.shape[0]
    experts_all = lax.axis_size("expert") * local_count
    other_bound = min(
        token_count,
        ((topk_width - 1) * token_count + experts_all - 3) // (experts_all - 2) * 3 // 2,
    )
    favoured_bound = token_count * 9 // 16
    slot_bound = max(favoured_bound, other_bound)
    buffer_rows = experts_all * slot_bound

    flat_ids = expert_ids.reshape(-1)
    one_hot = (flat_ids[:, None] == jnp.arange(experts_all, dtype=jnp.int32)[None, :]).astype(
        jnp.int32
    )
    earlier = jnp.cumsum(one_hot, axis=0) - one_hot
    slot_of = jnp.sum(earlier * one_hot, axis=1)
    places = (flat_ids * slot_bound + slot_of).reshape(token_count, topk_width)

    hit = (
        places[:, :, None] == jnp.arange(buffer_rows, dtype=jnp.int32)[None, None, :]
    ).reshape(token_count, topk_width, experts_all, slot_bound)
    pick = jnp.any(hit, axis=1).astype(jnp.bfloat16)
    small = slot_bound // 9
    answered = jnp.zeros((experts_all, slot_bound, features), jnp.bfloat16)
    for begin, end in ((0, slot_bound - small), (slot_bound - small, slot_bound)):
        outgoing = jnp.einsum(
            "tes,td->esd", pick[:, :, begin:end], tokens, preferred_element_type=jnp.float32
        ).astype(jnp.bfloat16)
        received = lax.all_to_all(outgoing, "expert", split_axis=0, concat_axis=0, tiled=True)
        answered = expert_blocks(
            received, w_gate[0], w_up[0], w_down[0], 4, answered, begin // (end - begin)
        )
    returned = lax.all_to_all(answered, "expert", split_axis=0, concat_axis=0, tiled=True)

    stacked = jnp.stack(
        [
            jnp.sum(jnp.where(hit, part.astype(jnp.float32)[:, :, None, None], 0.0), axis=1)
            for part in split_bf16(gate_values)
        ]
    ).astype(jnp.bfloat16)
    terms = jnp.einsum("ptes,esd->ptd", stacked, returned, preferred_element_type=jnp.float32)
    summed = jnp.sum(terms, axis=0)
    return summed.astype(jnp.bfloat16)


def solution(mesh):
    placed = (
        P(("dp", "expert"), None),
        P(("dp", "expert"), None),
        P(("dp", "expert"), None),
        P("expert", None, None),
        P("expert", None, None),
        P("expert", None, None),
    )
    return jax.shard_map(
        shards, mesh=mesh, in_specs=placed, out_specs=P(("dp", "expert"), None), check_vma=False
    )
```

```python
import functools

import jax
import jax.numpy as jnp
from jax import lax
from jax.experimental import pallas as pl
from jax.experimental.pallas import tpu as pltpu
from jax.sharding import PartitionSpec as P

MESH = pl.DeviceIdType.MESH


def exchange_kernel(n, x_ref, y_ref, send_sem, recv_sem, local_sem):
    me = lax.axis_index("expert")
    barrier = pltpu.get_barrier_semaphore()

    def greet(k, carry):
        pl.semaphore_signal(
            barrier, inc=1, device_id={"expert": lax.rem(me + k, n)}, device_id_type=MESH
        )
        return carry

    lax.fori_loop(1, n, greet, 0)
    pl.semaphore_wait(barrier, n - 1)
    local = pltpu.make_async_copy(x_ref.at[me], y_ref.at[me], local_sem)
    local.start()

    def remote(k):
        target = lax.rem(me + k, n)
        return pltpu.make_async_remote_copy(
            src_ref=x_ref.at[target],
            dst_ref=y_ref.at[me],
            send_sem=send_sem.at[k],
            recv_sem=recv_sem.at[k],
            device_id={"expert": target},
            device_id_type=MESH,
        )

    def start(k, carry):
        remote(k).start()
        return carry

    def finish(k, carry):
        remote(k).wait()
        return carry

    lax.fori_loop(1, n, start, 0)
    lax.fori_loop(1, n, finish, 0)
    local.wait()


def exchange(blocks, collective_id):
    n = lax.axis_size("expert")
    return pl.pallas_call(
        functools.partial(exchange_kernel, n),
        out_shape=jax.ShapeDtypeStruct(blocks.shape, blocks.dtype),
        in_specs=[pl.BlockSpec(memory_space=pl.ANY)],
        out_specs=pl.BlockSpec(memory_space=pl.ANY),
        scratch_shapes=[
            pltpu.SemaphoreType.DMA((n,)),
            pltpu.SemaphoreType.DMA((n,)),
            pltpu.SemaphoreType.DMA,
        ],
        compiler_params=pltpu.CompilerParams(collective_id=collective_id, has_side_effects=True),
    )(blocks)


def expert_apply(row_block, gate_matrix, up_matrix, down_matrix):
    gate_part = jnp.dot(row_block, gate_matrix, preferred_element_type=jnp.float32)
    up_part = jnp.dot(row_block, up_matrix, preferred_element_type=jnp.float32)
    hidden = (jax.nn.silu(gate_part) * up_part).astype(jnp.bfloat16)
    return jnp.dot(hidden, down_matrix, preferred_element_type=jnp.float32).astype(jnp.bfloat16)


def ffn_kernel(x_ref, gate_ref, up_ref, down_ref, out_ref):
    sources, slots, features = x_ref.shape
    rows = x_ref[...].reshape(sources * slots, features)
    out_ref[...] = expert_apply(rows, gate_ref[...], up_ref[...], down_ref[...]).reshape(
        sources, slots, features
    )


def expert_blocks(received, gate_matrix, up_matrix, down_matrix, slots, per_step, slot_block):
    sources, _, features = received.shape
    hidden = gate_matrix.shape[1]
    return pl.pallas_call(
        ffn_kernel,
        out_shape=jax.ShapeDtypeStruct((sources, slots, features), received.dtype),
        grid=(sources // per_step,),
        in_specs=[
            pl.BlockSpec((per_step, slots, features), lambda i: (i, slot_block, 0)),
            pl.BlockSpec((features, hidden), lambda i: (0, 0)),
            pl.BlockSpec((features, hidden), lambda i: (0, 0)),
            pl.BlockSpec((hidden, features), lambda i: (0, 0)),
        ],
        out_specs=pl.BlockSpec((per_step, slots, features), lambda i: (i, 0, 0)),
        compiler_params=pltpu.CompilerParams(vmem_limit_bytes=60 * 1024 * 1024),
        cost_estimate=pl.CostEstimate(
            flops=6 * sources * slots * features * hidden,
            transcendentals=sources * slots * hidden,
            bytes_accessed=2 * (2 * sources * slots * features + 3 * features * hidden),
        ),
    )(received, gate_matrix, up_matrix, down_matrix)


def split_bf16(values):
    first = lax.reduce_precision(values, exponent_bits=8, mantissa_bits=7)
    second = values - first
    return tuple(part.astype(jnp.bfloat16) for part in (first, second))


def shards(tokens, expert_ids, gate_values, w_gate, w_up, w_down):
    token_count, features = tokens.shape
    topk_width = expert_ids.shape[1]
    local_count = w_gate.shape[0]
    experts_all = lax.axis_size("expert") * local_count
    other_bound = min(
        token_count,
        ((topk_width - 1) * token_count + experts_all - 3) // (experts_all - 2) * 3 // 2,
    )
    favoured_bound = token_count * 9 // 16
    slot_bound = max(favoured_bound, other_bound)
    buffer_rows = experts_all * slot_bound

    flat_ids = expert_ids.reshape(-1)
    one_hot = (flat_ids[:, None] == jnp.arange(experts_all, dtype=jnp.int32)[None, :]).astype(
        jnp.int32
    )
    earlier = jnp.cumsum(one_hot, axis=0) - one_hot
    slot_of = jnp.sum(earlier * one_hot, axis=1)
    places = (flat_ids * slot_bound + slot_of).reshape(token_count, topk_width)

    hit = (
        places[:, :, None] == jnp.arange(buffer_rows, dtype=jnp.int32)[None, None, :]
    ).reshape(token_count, topk_width, experts_all, slot_bound)
    pick = jnp.any(hit, axis=1).astype(jnp.bfloat16)
    outgoing = jnp.einsum(
        "tes,td->esd", pick, tokens, preferred_element_type=jnp.float32
    ).astype(jnp.bfloat16)
    received = lax.all_to_all(outgoing, "expert", split_axis=0, concat_axis=0, tiled=True)

    large = slot_bound - slot_bound // 9
    weight_parts = split_bf16(gate_values)
    summed = None
    for begin, end in ((large, slot_bound), (0, large)):
        size = end - begin
        per_step = 4 if begin == 0 else experts_all
        answered = expert_blocks(
            received, w_gate[0], w_up[0], w_down[0], size, per_step, begin // size
        )
        returned = lax.all_to_all(answered, "expert", split_axis=0, concat_axis=0, tiled=True)
        stacked = jnp.stack(
            [
                jnp.sum(
                    jnp.where(
                        hit[:, :, :, begin:end], part.astype(jnp.float32)[:, :, None, None], 0.0
                    ),
                    axis=1,
                )
                for part in weight_parts
            ]
        ).astype(jnp.bfloat16)
        terms = jnp.einsum("ptes,esd->ptd", stacked, returned, preferred_element_type=jnp.float32)
        term = jnp.sum(terms, axis=0)
        summed = term if summed is None else summed + term
    return summed.astype(jnp.bfloat16)


def solution(mesh):
    placed = (
        P(("dp", "expert"), None),
        P(("dp", "expert"), None),
        P(("dp", "expert"), None),
        P("expert", None, None),
        P("expert", None, None),
        P("expert", None, None),
    )
    return jax.shard_map(
        shards, mesh=mesh, in_specs=placed, out_specs=P(("dp", "expert"), None), check_vma=False
    )
```

```python
import functools

import jax
import jax.numpy as jnp
from jax import lax
from jax.experimental import pallas as pl
from jax.experimental.pallas import tpu as pltpu
from jax.sharding import PartitionSpec as P

MESH = pl.DeviceIdType.MESH


def expert_apply(row_block, gate_matrix, up_matrix, down_matrix):
    gate_part = jnp.dot(row_block, gate_matrix, preferred_element_type=jnp.float32)
    up_part = jnp.dot(row_block, up_matrix, preferred_element_type=jnp.float32)
    hidden = (jax.nn.silu(gate_part) * up_part).astype(jnp.bfloat16)
    return jnp.dot(hidden, down_matrix, preferred_element_type=jnp.float32).astype(jnp.bfloat16)


def ffn_kernel(
    n, small_ref, large_ref, gate_ref, up_ref, down_ref, large_out, small_out,
    held, send_sem, recv_sem, local_sem,
):
    step = pl.program_id(0)
    me = lax.axis_index("expert")
    local = pltpu.make_async_copy(held.at[me], small_out.at[me], local_sem)

    def remote(k):
        target = lax.rem(me + k, n)
        return pltpu.make_async_remote_copy(
            src_ref=held.at[target],
            dst_ref=small_out.at[me],
            send_sem=send_sem.at[k],
            recv_sem=recv_sem.at[k],
            device_id={"expert": target},
            device_id_type=MESH,
        )

    def start(k, carry):
        remote(k).start()
        return carry

    def finish(k, carry):
        remote(k).wait()
        return carry

    @pl.when(step == 0)
    def _():
        barrier = pltpu.get_barrier_semaphore()

        def greet(k, carry):
            pl.semaphore_signal(
                barrier, inc=1, device_id={"expert": lax.rem(me + k, n)}, device_id_type=MESH
            )
            return carry

        lax.fori_loop(1, n, greet, 0)
        pl.semaphore_wait(barrier, n - 1)
        sources, slots, features = small_ref.shape
        rows = small_ref[...].reshape(sources * slots, features)
        held[...] = expert_apply(rows, gate_ref[...], up_ref[...], down_ref[...]).reshape(
            sources, slots, features
        )
        local.start()
        lax.fori_loop(1, n, start, 0)

    sources, slots, features = large_ref.shape
    rows = large_ref[...].reshape(sources * slots, features)
    large_out[...] = expert_apply(rows, gate_ref[...], up_ref[...], down_ref[...]).reshape(
        sources, slots, features
    )

    @pl.when(step == pl.num_programs(0) - 1)
    def _():
        lax.fori_loop(1, n, finish, 0)
        local.wait()


def expert_blocks(received, gate_matrix, up_matrix, down_matrix, large, per_step):
    n = lax.axis_size("expert")
    sources, slot_bound, features = received.shape
    small = slot_bound - large
    hidden = gate_matrix.shape[1]
    return pl.pallas_call(
        functools.partial(ffn_kernel, n),
        out_shape=(
            jax.ShapeDtypeStruct((sources, large, features), received.dtype),
            jax.ShapeDtypeStruct((sources, small, features), received.dtype),
        ),
        grid=(sources // per_step,),
        in_specs=[
            pl.BlockSpec((sources, small, features), lambda i: (0, large // small, 0)),
            pl.BlockSpec((per_step, large, features), lambda i: (i, 0, 0)),
            pl.BlockSpec((features, hidden), lambda i: (0, 0)),
            pl.BlockSpec((features, hidden), lambda i: (0, 0)),
            pl.BlockSpec((hidden, features), lambda i: (0, 0)),
        ],
        out_specs=(
            pl.BlockSpec((per_step, large, features), lambda i: (i, 0, 0)),
            pl.BlockSpec(memory_space=pl.ANY),
        ),
        scratch_shapes=[
            pltpu.VMEM((sources, small, features), received.dtype),
            pltpu.SemaphoreType.DMA((n,)),
            pltpu.SemaphoreType.DMA((n,)),
            pltpu.SemaphoreType.DMA,
        ],
        compiler_params=pltpu.CompilerParams(
            collective_id=0, has_side_effects=True, vmem_limit_bytes=60 * 1024 * 1024
        ),
        cost_estimate=pl.CostEstimate(
            flops=6 * sources * slot_bound * features * hidden,
            transcendentals=sources * slot_bound * hidden,
            bytes_accessed=2 * (2 * sources * slot_bound * features + 3 * features * hidden),
        ),
    )(received, received, gate_matrix, up_matrix, down_matrix)


def split_bf16(values):
    first = lax.reduce_precision(values, exponent_bits=8, mantissa_bits=7)
    second = values - first
    return tuple(part.astype(jnp.bfloat16) for part in (first, second))


def shards(tokens, expert_ids, gate_values, w_gate, w_up, w_down):
    token_count, features = tokens.shape
    topk_width = expert_ids.shape[1]
    local_count = w_gate.shape[0]
    experts_all = lax.axis_size("expert") * local_count
    other_bound = min(
        token_count,
        ((topk_width - 1) * token_count + experts_all - 3) // (experts_all - 2) * 3 // 2,
    )
    favoured_bound = token_count * 9 // 16
    slot_bound = max(favoured_bound, other_bound)
    buffer_rows = experts_all * slot_bound

    flat_ids = expert_ids.reshape(-1)
    one_hot = (flat_ids[:, None] == jnp.arange(experts_all, dtype=jnp.int32)[None, :]).astype(
        jnp.int32
    )
    earlier = jnp.cumsum(one_hot, axis=0) - one_hot
    slot_of = jnp.sum(earlier * one_hot, axis=1)
    places = (flat_ids * slot_bound + slot_of).reshape(token_count, topk_width)

    hit = (
        places[:, :, None] == jnp.arange(buffer_rows, dtype=jnp.int32)[None, None, :]
    ).reshape(token_count, topk_width, experts_all, slot_bound)
    pick = jnp.any(hit, axis=1).astype(jnp.bfloat16)
    outgoing = jnp.einsum(
        "tes,td->esd", pick, tokens, preferred_element_type=jnp.float32
    ).astype(jnp.bfloat16)
    received = lax.all_to_all(outgoing, "expert", split_axis=0, concat_axis=0, tiled=True)

    large = slot_bound - slot_bound // 9
    answered, returned_small = expert_blocks(received, w_gate[0], w_up[0], w_down[0], large, 4)
    returned_large = lax.all_to_all(answered, "expert", split_axis=0, concat_axis=0, tiled=True)
    weight_parts = split_bf16(gate_values)
    summed = None
    for begin, end, returned in ((large, slot_bound, returned_small), (0, large, returned_large)):
        stacked = jnp.stack(
            [
                jnp.sum(
                    jnp.where(
                        hit[:, :, :, begin:end], part.astype(jnp.float32)[:, :, None, None], 0.0
                    ),
                    axis=1,
                )
                for part in weight_parts
            ]
        ).astype(jnp.bfloat16)
        terms = jnp.einsum("ptes,esd->ptd", stacked, returned, preferred_element_type=jnp.float32)
        term = jnp.sum(terms, axis=0)
        summed = term if summed is None else summed + term
    return summed.astype(jnp.bfloat16)


def solution(mesh):
    placed = (
        P(("dp", "expert"), None),
        P(("dp", "expert"), None),
        P(("dp", "expert"), None),
        P("expert", None, None),
        P("expert", None, None),
        P("expert", None, None),
    )
    return jax.shard_map(
        shards, mesh=mesh, in_specs=placed, out_specs=P(("dp", "expert"), None), check_vma=False
    )
```

```python
import functools

import jax
import jax.numpy as jnp
from jax import lax
from jax.experimental import pallas as pl
from jax.experimental.pallas import tpu as pltpu
from jax.sharding import PartitionSpec as P

MESH = pl.DeviceIdType.MESH


def expert_apply(row_block, gate_matrix, up_matrix, down_matrix):
    gate_part = jnp.dot(row_block, gate_matrix, preferred_element_type=jnp.float32)
    up_part = jnp.dot(row_block, up_matrix, preferred_element_type=jnp.float32)
    hidden = (jax.nn.silu(gate_part) * up_part).astype(jnp.bfloat16)
    return jnp.dot(hidden, down_matrix, preferred_element_type=jnp.float32).astype(jnp.bfloat16)


def ffn_kernel(
    n, small_ref, large_ref, gate_ref, up_ref, down_ref, large_out, small_out,
    held, send_sem, recv_sem, local_sem,
):
    step = pl.program_id(0)
    me = lax.axis_index("expert")
    local = pltpu.make_async_copy(held.at[me], small_out.at[me], local_sem)

    def remote(k):
        target = lax.rem(me + k, n)
        return pltpu.make_async_remote_copy(
            src_ref=held.at[target],
            dst_ref=small_out.at[me],
            send_sem=send_sem.at[k],
            recv_sem=recv_sem.at[k],
            device_id={"expert": target},
            device_id_type=MESH,
        )

    def start(k, carry):
        remote(k).start()
        return carry

    def finish(k, carry):
        remote(k).wait()
        return carry

    @pl.when(step == 0)
    def _():
        barrier = pltpu.get_barrier_semaphore()

        def greet(k, carry):
            pl.semaphore_signal(
                barrier, inc=1, device_id={"expert": lax.rem(me + k, n)}, device_id_type=MESH
            )
            return carry

        lax.fori_loop(1, n, greet, 0)
        pl.semaphore_wait(barrier, n - 1)
        sources, slots, features = small_ref.shape
        rows = small_ref[...].reshape(sources * slots, features)
        held[...] = expert_apply(rows, gate_ref[...], up_ref[...], down_ref[...]).reshape(
            sources, slots, features
        )
        local.start()
        lax.fori_loop(1, n, start, 0)

    sources, slots, features = large_ref.shape
    rows = large_ref[...].reshape(sources * slots, features)
    large_out[...] = expert_apply(rows, gate_ref[...], up_ref[...], down_ref[...]).reshape(
        sources, slots, features
    )

    @pl.when(step == pl.num_programs(0) - 1)
    def _():
        lax.fori_loop(1, n, finish, 0)
        local.wait()


def expert_blocks(received, gate_matrix, up_matrix, down_matrix, large, per_step):
    n = lax.axis_size("expert")
    sources, slot_bound, features = received.shape
    small = slot_bound - large
    hidden = gate_matrix.shape[1]
    return pl.pallas_call(
        functools.partial(ffn_kernel, n),
        out_shape=(
            jax.ShapeDtypeStruct((sources, large, features), received.dtype),
            jax.ShapeDtypeStruct((sources, small, features), received.dtype),
        ),
        grid=(sources // per_step,),
        in_specs=[
            pl.BlockSpec((sources, small, features), lambda i: (0, large // small, 0)),
            pl.BlockSpec((per_step, large, features), lambda i: (i, 0, 0)),
            pl.BlockSpec((features, hidden), lambda i: (0, 0)),
            pl.BlockSpec((features, hidden), lambda i: (0, 0)),
            pl.BlockSpec((hidden, features), lambda i: (0, 0)),
        ],
        out_specs=(
            pl.BlockSpec((per_step, large, features), lambda i: (i, 0, 0)),
            pl.BlockSpec(memory_space=pl.ANY),
        ),
        scratch_shapes=[
            pltpu.VMEM((sources, small, features), received.dtype),
            pltpu.SemaphoreType.DMA((n,)),
            pltpu.SemaphoreType.DMA((n,)),
            pltpu.SemaphoreType.DMA,
        ],
        compiler_params=pltpu.CompilerParams(
            collective_id=0, has_side_effects=True, vmem_limit_bytes=60 * 1024 * 1024
        ),
        cost_estimate=pl.CostEstimate(
            flops=6 * sources * slot_bound * features * hidden,
            transcendentals=sources * slot_bound * hidden,
            bytes_accessed=2 * (2 * sources * slot_bound * features + 3 * features * hidden),
        ),
    )(received, received, gate_matrix, up_matrix, down_matrix)


def combine_kernel(weights_ref, returned_ref, partial_ref, out_ref):
    total = partial_ref[...]
    for part in range(weights_ref.shape[0]):
        total = total + jnp.dot(
            weights_ref[part], returned_ref[...], preferred_element_type=jnp.float32
        )
    out_ref[...] = total.astype(out_ref.dtype)


def combine(weights, returned, partial, columns):
    parts, tokens, rows = weights.shape
    features = returned.shape[1]
    return pl.pallas_call(
        combine_kernel,
        out_shape=jax.ShapeDtypeStruct((tokens, features), jnp.bfloat16),
        grid=(features // columns,),
        in_specs=[
            pl.BlockSpec((parts, tokens, rows), lambda j: (0, 0, 0)),
            pl.BlockSpec((rows, columns), lambda j: (0, j)),
            pl.BlockSpec((tokens, columns), lambda j: (0, j)),
        ],
        out_specs=pl.BlockSpec((tokens, columns), lambda j: (0, j)),
        cost_estimate=pl.CostEstimate(
            flops=2 * parts * tokens * rows * features,
            transcendentals=0,
            bytes_accessed=2 * rows * features + 6 * tokens * features,
        ),
    )(weights, returned, partial)


def split_bf16(values):
    first = lax.reduce_precision(values, exponent_bits=8, mantissa_bits=7)
    second = values - first
    return tuple(part.astype(jnp.bfloat16) for part in (first, second))


def shards(tokens, expert_ids, gate_values, w_gate, w_up, w_down):
    token_count, features = tokens.shape
    topk_width = expert_ids.shape[1]
    local_count = w_gate.shape[0]
    experts_all = lax.axis_size("expert") * local_count
    other_bound = min(
        token_count,
        ((topk_width - 1) * token_count + experts_all - 3) // (experts_all - 2) * 3 // 2,
    )
    favoured_bound = token_count * 9 // 16
    slot_bound = max(favoured_bound, other_bound)
    buffer_rows = experts_all * slot_bound

    flat_ids = expert_ids.reshape(-1)
    one_hot = (flat_ids[:, None] == jnp.arange(experts_all, dtype=jnp.int32)[None, :]).astype(
        jnp.int32
    )
    earlier = jnp.cumsum(one_hot, axis=0) - one_hot
    slot_of = jnp.sum(earlier * one_hot, axis=1)
    places = (flat_ids * slot_bound + slot_of).reshape(token_count, topk_width)

    hit = (
        places[:, :, None] == jnp.arange(buffer_rows, dtype=jnp.int32)[None, None, :]
    ).reshape(token_count, topk_width, experts_all, slot_bound)
    pick = jnp.any(hit, axis=1).astype(jnp.bfloat16)
    outgoing = jnp.einsum(
        "tes,td->esd", pick, tokens, preferred_element_type=jnp.float32
    ).astype(jnp.bfloat16)
    received = lax.all_to_all(outgoing, "expert", split_axis=0, concat_axis=0, tiled=True)

    large = slot_bound - slot_bound // 9
    answered, returned_small = expert_blocks(received, w_gate[0], w_up[0], w_down[0], large, 4)
    returned_large = lax.all_to_all(answered, "expert", split_axis=0, concat_axis=0, tiled=True)
    weight_parts = split_bf16(gate_values)
    stacked = [
        jnp.stack(
            [
                jnp.sum(
                    jnp.where(
                        hit[:, :, :, begin:end], part.astype(jnp.float32)[:, :, None, None], 0.0
                    ),
                    axis=1,
                )
                for part in weight_parts
            ]
        ).astype(jnp.bfloat16)
        for begin, end in ((large, slot_bound), (0, large))
    ]
    small_terms = jnp.einsum(
        "ptes,esd->ptd", stacked[0], returned_small, preferred_element_type=jnp.float32
    )
    parts = len(weight_parts)
    return combine(
        stacked[1].reshape(parts, token_count, experts_all * large),
        returned_large.reshape(experts_all * large, features),
        jnp.sum(small_terms, axis=0),
        512,
    )


def solution(mesh):
    placed = (
        P(("dp", "expert"), None),
        P(("dp", "expert"), None),
        P(("dp", "expert"), None),
        P("expert", None, None),
        P("expert", None, None),
        P("expert", None, None),
    )
    return jax.shard_map(
        shards, mesh=mesh, in_specs=placed, out_specs=P(("dp", "expert"), None), check_vma=False
    )
```

```python
import functools

import jax
import jax.numpy as jnp
from jax import lax
from jax.experimental import pallas as pl
from jax.experimental.pallas import tpu as pltpu
from jax.sharding import PartitionSpec as P

MESH = pl.DeviceIdType.MESH


def expert_apply(row_block, gate_matrix, up_matrix, down_matrix):
    gate_part = jnp.dot(row_block, gate_matrix, preferred_element_type=jnp.float32)
    up_part = jnp.dot(row_block, up_matrix, preferred_element_type=jnp.float32)
    hidden = (jax.nn.silu(gate_part) * up_part).astype(jnp.bfloat16)
    return jnp.dot(hidden, down_matrix, preferred_element_type=jnp.float32).astype(jnp.bfloat16)


def ffn_kernel(
    n, small_ref, large_ref, gate_ref, up_ref, down_ref, large_out, small_out,
    held, send_sem, recv_sem, local_sem,
):
    step = pl.program_id(0)
    me = lax.axis_index("expert")
    local = pltpu.make_async_copy(held.at[me], small_out.at[me], local_sem)

    def remote(k):
        target = lax.rem(me + k, n)
        return pltpu.make_async_remote_copy(
            src_ref=held.at[target],
            dst_ref=small_out.at[me],
            send_sem=send_sem.at[k],
            recv_sem=recv_sem.at[k],
            device_id={"expert": target},
            device_id_type=MESH,
        )

    def start(k, carry):
        remote(k).start()
        return carry

    def finish(k, carry):
        remote(k).wait()
        return carry

    @pl.when(step == 0)
    def _():
        barrier = pltpu.get_barrier_semaphore()

        def greet(k, carry):
            pl.semaphore_signal(
                barrier, inc=1, device_id={"expert": lax.rem(me + k, n)}, device_id_type=MESH
            )
            return carry

        lax.fori_loop(1, n, greet, 0)
        pl.semaphore_wait(barrier, n - 1)
        sources, slots, features = small_ref.shape
        rows = small_ref[...].reshape(sources * slots, features)
        held[...] = expert_apply(rows, gate_ref[...], up_ref[...], down_ref[...]).reshape(
            sources, slots, features
        )
        local.start()
        lax.fori_loop(1, n, start, 0)

    sources, slots, features = large_ref.shape
    rows = large_ref[...].reshape(sources * slots, features)
    large_out[...] = expert_apply(rows, gate_ref[...], up_ref[...], down_ref[...]).reshape(
        sources, slots, features
    )

    @pl.when(step == pl.num_programs(0) - 1)
    def _():
        lax.fori_loop(1, n, finish, 0)
        local.wait()


def expert_blocks(received, gate_matrix, up_matrix, down_matrix, large, per_step):
    n = lax.axis_size("expert")
    sources, slot_bound, features = received.shape
    small = slot_bound - large
    hidden = gate_matrix.shape[1]
    return pl.pallas_call(
        functools.partial(ffn_kernel, n),
        out_shape=(
            jax.ShapeDtypeStruct((sources, large, features), received.dtype),
            jax.ShapeDtypeStruct((sources, small, features), received.dtype),
        ),
        grid=(sources // per_step,),
        in_specs=[
            pl.BlockSpec((sources, small, features), lambda i: (0, large // small, 0)),
            pl.BlockSpec((per_step, large, features), lambda i: (i, 0, 0)),
            pl.BlockSpec((features, hidden), lambda i: (0, 0)),
            pl.BlockSpec((features, hidden), lambda i: (0, 0)),
            pl.BlockSpec((hidden, features), lambda i: (0, 0)),
        ],
        out_specs=(
            pl.BlockSpec((per_step, large, features), lambda i: (i, 0, 0)),
            pl.BlockSpec(memory_space=pl.ANY),
        ),
        scratch_shapes=[
            pltpu.VMEM((sources, small, features), received.dtype),
            pltpu.SemaphoreType.DMA((n,)),
            pltpu.SemaphoreType.DMA((n,)),
            pltpu.SemaphoreType.DMA,
        ],
        compiler_params=pltpu.CompilerParams(
            collective_id=0, has_side_effects=True, vmem_limit_bytes=60 * 1024 * 1024
        ),
        cost_estimate=pl.CostEstimate(
            flops=6 * sources * slot_bound * features * hidden,
            transcendentals=sources * slot_bound * hidden,
            bytes_accessed=2 * (2 * sources * slot_bound * features + 3 * features * hidden),
        ),
    )(received, received, gate_matrix, up_matrix, down_matrix)


def split_bf16(values):
    first = lax.reduce_precision(values, exponent_bits=8, mantissa_bits=7)
    second = values - first
    return tuple(part.astype(jnp.bfloat16) for part in (first, second))


def shards(tokens, expert_ids, gate_values, w_gate, w_up, w_down):
    token_count, features = tokens.shape
    topk_width = expert_ids.shape[1]
    local_count = w_gate.shape[0]
    experts_all = lax.axis_size("expert") * local_count
    other_bound = min(
        token_count,
        ((topk_width - 1) * token_count + experts_all - 3) // (experts_all - 2) * 3 // 2,
    )
    favoured_bound = token_count * 9 // 16
    slot_bound = max(favoured_bound, other_bound)
    buffer_rows = experts_all * slot_bound

    flat_ids = expert_ids.reshape(-1)
    one_hot = (flat_ids[:, None] == jnp.arange(experts_all, dtype=jnp.int32)[None, :]).astype(
        jnp.bfloat16
    )
    pair_count = flat_ids.shape[0]
    pair_index = jnp.arange(pair_count, dtype=jnp.int32)
    before = (pair_index[:, None] > pair_index[None, :]).astype(jnp.bfloat16)
    earlier = jnp.dot(before, one_hot, preferred_element_type=jnp.float32)
    slot_of = jnp.sum(earlier * one_hot.astype(jnp.float32), axis=1).astype(jnp.int32)
    places = (flat_ids * slot_bound + slot_of).reshape(token_count, topk_width)

    hit = (
        places[:, :, None] == jnp.arange(buffer_rows, dtype=jnp.int32)[None, None, :]
    ).reshape(token_count, topk_width, experts_all, slot_bound)
    pick = jnp.any(hit, axis=1).astype(jnp.bfloat16)
    outgoing = jnp.einsum(
        "tes,td->esd", pick, tokens, preferred_element_type=jnp.float32
    ).astype(jnp.bfloat16)
    received = lax.all_to_all(outgoing, "expert", split_axis=0, concat_axis=0, tiled=True)

    large = slot_bound - slot_bound // 9
    answered, returned_small = expert_blocks(received, w_gate[0], w_up[0], w_down[0], large, 4)
    returned_large = lax.all_to_all(answered, "expert", split_axis=0, concat_axis=0, tiled=True)
    weight_parts = split_bf16(gate_values)
    summed = None
    for begin, end, returned in ((large, slot_bound, returned_small), (0, large, returned_large)):
        stacked = jnp.stack(
            [
                jnp.sum(
                    jnp.where(
                        hit[:, :, :, begin:end], part.astype(jnp.float32)[:, :, None, None], 0.0
                    ),
                    axis=1,
                )
                for part in weight_parts
            ]
        ).astype(jnp.bfloat16)
        terms = jnp.einsum("ptes,esd->ptd", stacked, returned, preferred_element_type=jnp.float32)
        term = jnp.sum(terms, axis=0)
        summed = term if summed is None else summed + term
    return summed.astype(jnp.bfloat16)


def solution(mesh):
    placed = (
        P(("dp", "expert"), None),
        P(("dp", "expert"), None),
        P(("dp", "expert"), None),
        P("expert", None, None),
        P("expert", None, None),
        P("expert", None, None),
    )
    return jax.shard_map(
        shards, mesh=mesh, in_specs=placed, out_specs=P(("dp", "expert"), None), check_vma=False
    )
```

```python
import functools

import jax
import jax.numpy as jnp
from jax import lax
from jax.experimental import pallas as pl
from jax.experimental.pallas import tpu as pltpu
from jax.sharding import PartitionSpec as P

MESH = pl.DeviceIdType.MESH


def expert_apply(row_block, gate_matrix, up_matrix, down_matrix):
    gate_part = jnp.dot(row_block, gate_matrix, preferred_element_type=jnp.float32)
    up_part = jnp.dot(row_block, up_matrix, preferred_element_type=jnp.float32)
    hidden = (jax.nn.silu(gate_part) * up_part).astype(jnp.bfloat16)
    return jnp.dot(hidden, down_matrix, preferred_element_type=jnp.float32).astype(jnp.bfloat16)


def ffn_kernel(
    n, small_ref, large_ref, gate_hbm, up_hbm, down_hbm, large_out, small_out,
    held, gate_ref, up_ref, down_ref, send_sem, recv_sem, local_sem, weight_sem,
):
    step = pl.program_id(0)
    me = lax.axis_index("expert")
    local = pltpu.make_async_copy(held.at[me], small_out.at[me], local_sem)

    def remote(k):
        target = lax.rem(me + k, n)
        return pltpu.make_async_remote_copy(
            src_ref=held.at[target],
            dst_ref=small_out.at[me],
            send_sem=send_sem.at[k],
            recv_sem=recv_sem.at[k],
            device_id={"expert": target},
            device_id_type=MESH,
        )

    def start(k, carry):
        remote(k).start()
        return carry

    def finish(k, carry):
        remote(k).wait()
        return carry

    fetches = [
        pltpu.make_async_copy(source, target, weight_sem.at[index])
        for index, (source, target) in enumerate(
            ((gate_hbm, gate_ref), (up_hbm, up_ref), (down_hbm, down_ref))
        )
    ]

    @pl.when(step == 0)
    def _():
        for fetch in fetches:
            fetch.start()
        barrier = pltpu.get_barrier_semaphore()

        def greet(k, carry):
            pl.semaphore_signal(
                barrier, inc=1, device_id={"expert": lax.rem(me + k, n)}, device_id_type=MESH
            )
            return carry

        lax.fori_loop(1, n, greet, 0)
        pl.semaphore_wait(barrier, n - 1)
        sources, slots, features = small_ref.shape
        rows = small_ref[...].reshape(sources * slots, features)
        fetches[0].wait()
        gate_part = jnp.dot(rows, gate_ref[...], preferred_element_type=jnp.float32)
        fetches[1].wait()
        up_part = jnp.dot(rows, up_ref[...], preferred_element_type=jnp.float32)
        hidden = (jax.nn.silu(gate_part) * up_part).astype(jnp.bfloat16)
        fetches[2].wait()
        held[...] = (
            jnp.dot(hidden, down_ref[...], preferred_element_type=jnp.float32)
            .astype(jnp.bfloat16)
            .reshape(sources, slots, features)
        )
        local.start()
        lax.fori_loop(1, n, start, 0)

    sources, slots, features = large_ref.shape
    rows = large_ref[...].reshape(sources * slots, features)
    large_out[...] = expert_apply(rows, gate_ref[...], up_ref[...], down_ref[...]).reshape(
        sources, slots, features
    )

    @pl.when(step == pl.num_programs(0) - 1)
    def _():
        lax.fori_loop(1, n, finish, 0)
        local.wait()


def expert_blocks(received, gate_matrix, up_matrix, down_matrix, large, per_step):
    n = lax.axis_size("expert")
    sources, slot_bound, features = received.shape
    small = slot_bound - large
    hidden = gate_matrix.shape[1]
    return pl.pallas_call(
        functools.partial(ffn_kernel, n),
        out_shape=(
            jax.ShapeDtypeStruct((sources, large, features), received.dtype),
            jax.ShapeDtypeStruct((sources, small, features), received.dtype),
        ),
        grid=(sources // per_step,),
        in_specs=[
            pl.BlockSpec((sources, small, features), lambda i: (0, large // small, 0)),
            pl.BlockSpec((per_step, large, features), lambda i: (i, 0, 0)),
            pl.BlockSpec(memory_space=pl.ANY),
            pl.BlockSpec(memory_space=pl.ANY),
            pl.BlockSpec(memory_space=pl.ANY),
        ],
        out_specs=(
            pl.BlockSpec((per_step, large, features), lambda i: (i, 0, 0)),
            pl.BlockSpec(memory_space=pl.ANY),
        ),
        scratch_shapes=[
            pltpu.VMEM((sources, small, features), received.dtype),
            pltpu.VMEM(gate_matrix.shape, gate_matrix.dtype),
            pltpu.VMEM(up_matrix.shape, up_matrix.dtype),
            pltpu.VMEM(down_matrix.shape, down_matrix.dtype),
            pltpu.SemaphoreType.DMA((n,)),
            pltpu.SemaphoreType.DMA((n,)),
            pltpu.SemaphoreType.DMA,
            pltpu.SemaphoreType.DMA((3,)),
        ],
        compiler_params=pltpu.CompilerParams(
            collective_id=0, has_side_effects=True, vmem_limit_bytes=60 * 1024 * 1024
        ),
        cost_estimate=pl.CostEstimate(
            flops=6 * sources * slot_bound * features * hidden,
            transcendentals=sources * slot_bound * hidden,
            bytes_accessed=2 * (2 * sources * slot_bound * features + 3 * features * hidden),
        ),
    )(received, received, gate_matrix, up_matrix, down_matrix)


def split_bf16(values):
    first = lax.reduce_precision(values, exponent_bits=8, mantissa_bits=7)
    second = values - first
    return tuple(part.astype(jnp.bfloat16) for part in (first, second))


def shards(tokens, expert_ids, gate_values, w_gate, w_up, w_down):
    token_count, features = tokens.shape
    topk_width = expert_ids.shape[1]
    local_count = w_gate.shape[0]
    experts_all = lax.axis_size("expert") * local_count
    other_bound = min(
        token_count,
        ((topk_width - 1) * token_count + experts_all - 3) // (experts_all - 2) * 3 // 2,
    )
    favoured_bound = token_count * 9 // 16
    slot_bound = max(favoured_bound, other_bound)
    buffer_rows = experts_all * slot_bound

    flat_ids = expert_ids.reshape(-1)
    one_hot = (flat_ids[:, None] == jnp.arange(experts_all, dtype=jnp.int32)[None, :]).astype(
        jnp.bfloat16
    )
    pair_count = flat_ids.shape[0]
    pair_index = jnp.arange(pair_count, dtype=jnp.int32)
    before = (pair_index[:, None] > pair_index[None, :]).astype(jnp.bfloat16)
    earlier = jnp.dot(before, one_hot, preferred_element_type=jnp.float32)
    slot_of = jnp.sum(earlier * one_hot.astype(jnp.float32), axis=1).astype(jnp.int32)
    places = (flat_ids * slot_bound + slot_of).reshape(token_count, topk_width)

    hit = (
        places[:, :, None] == jnp.arange(buffer_rows, dtype=jnp.int32)[None, None, :]
    ).reshape(token_count, topk_width, experts_all, slot_bound)
    pick = jnp.any(hit, axis=1).astype(jnp.bfloat16)
    outgoing = jnp.einsum(
        "tes,td->esd", pick, tokens, preferred_element_type=jnp.float32
    ).astype(jnp.bfloat16)
    received = lax.all_to_all(outgoing, "expert", split_axis=0, concat_axis=0, tiled=True)

    large = slot_bound - slot_bound // 9
    answered, returned_small = expert_blocks(received, w_gate[0], w_up[0], w_down[0], large, 4)
    returned_large = lax.all_to_all(answered, "expert", split_axis=0, concat_axis=0, tiled=True)
    weight_parts = split_bf16(gate_values)
    summed = None
    for begin, end, returned in ((large, slot_bound, returned_small), (0, large, returned_large)):
        stacked = jnp.stack(
            [
                jnp.sum(
                    jnp.where(
                        hit[:, :, :, begin:end], part.astype(jnp.float32)[:, :, None, None], 0.0
                    ),
                    axis=1,
                )
                for part in weight_parts
            ]
        ).astype(jnp.bfloat16)
        terms = jnp.einsum("ptes,esd->ptd", stacked, returned, preferred_element_type=jnp.float32)
        term = jnp.sum(terms, axis=0)
        summed = term if summed is None else summed + term
    return summed.astype(jnp.bfloat16)


def solution(mesh):
    placed = (
        P(("dp", "expert"), None),
        P(("dp", "expert"), None),
        P(("dp", "expert"), None),
        P("expert", None, None),
        P("expert", None, None),
        P("expert", None, None),
    )
    return jax.shard_map(
        shards, mesh=mesh, in_specs=placed, out_specs=P(("dp", "expert"), None), check_vma=False
    )
```

```python
import functools

import jax
import jax.numpy as jnp
from jax import lax
from jax.experimental import pallas as pl
from jax.experimental.pallas import tpu as pltpu
from jax.sharding import PartitionSpec as P

MESH = pl.DeviceIdType.MESH


def expert_apply(row_block, gate_matrix, up_matrix, down_matrix):
    gate_part = jnp.dot(row_block, gate_matrix, preferred_element_type=jnp.float32)
    up_part = jnp.dot(row_block, up_matrix, preferred_element_type=jnp.float32)
    hidden = (jax.nn.silu(gate_part) * up_part).astype(jnp.bfloat16)
    return jnp.dot(hidden, down_matrix, preferred_element_type=jnp.float32).astype(jnp.bfloat16)


def ffn_kernel(
    n, small_ref, large_ref, gate_hbm, up_hbm, down_hbm, large_out, small_out,
    held, gate_ref, up_ref, down_ref, send_sem, recv_sem, local_sem, weight_sem,
):
    step = pl.program_id(0)
    me = lax.axis_index("expert")
    local = pltpu.make_async_copy(held.at[me], small_out.at[me], local_sem)

    def remote(k):
        target = lax.rem(me + k, n)
        return pltpu.make_async_remote_copy(
            src_ref=held.at[target],
            dst_ref=small_out.at[me],
            send_sem=send_sem.at[k],
            recv_sem=recv_sem.at[k],
            device_id={"expert": target},
            device_id_type=MESH,
        )

    def start(k, carry):
        remote(k).start()
        return carry

    def finish(k, carry):
        remote(k).wait()
        return carry

    fetches = [
        pltpu.make_async_copy(source, target, weight_sem.at[index])
        for index, (source, target) in enumerate(
            ((gate_hbm, gate_ref), (up_hbm, up_ref), (down_hbm, down_ref))
        )
    ]

    @pl.when(step == 0)
    def _():
        for fetch in fetches:
            fetch.start()
        barrier = pltpu.get_barrier_semaphore()

        def greet(k, carry):
            pl.semaphore_signal(
                barrier, inc=1, device_id={"expert": lax.rem(me + k, n)}, device_id_type=MESH
            )
            return carry

        lax.fori_loop(1, n, greet, 0)
        pl.semaphore_wait(barrier, n - 1)
        sources, slots, features = small_ref.shape
        rows = small_ref[...].reshape(sources * slots, features)
        fetches[0].wait()
        gate_part = jnp.dot(rows, gate_ref[...], preferred_element_type=jnp.float32)
        fetches[1].wait()
        up_part = jnp.dot(rows, up_ref[...], preferred_element_type=jnp.float32)
        hidden = (jax.nn.silu(gate_part) * up_part).astype(jnp.bfloat16)
        fetches[2].wait()
        held[...] = (
            jnp.dot(hidden, down_ref[...], preferred_element_type=jnp.float32)
            .astype(jnp.bfloat16)
            .reshape(sources, slots, features)
        )
        local.start()
        lax.fori_loop(1, n, start, 0)

    sources, slots, features = large_ref.shape
    rows = large_ref[...].reshape(sources * slots, features)
    large_out[...] = expert_apply(rows, gate_ref[...], up_ref[...], down_ref[...]).reshape(
        sources, slots, features
    )

    @pl.when(step == pl.num_programs(0) - 1)
    def _():
        lax.fori_loop(1, n, finish, 0)
        local.wait()


def expert_blocks(received, gate_matrix, up_matrix, down_matrix, large, per_step):
    n = lax.axis_size("expert")
    sources, slot_bound, features = received.shape
    small = slot_bound - large
    hidden = gate_matrix.shape[1]
    return pl.pallas_call(
        functools.partial(ffn_kernel, n),
        out_shape=(
            jax.ShapeDtypeStruct((sources, large, features), received.dtype),
            jax.ShapeDtypeStruct((sources, small, features), received.dtype),
        ),
        grid=(sources // per_step,),
        in_specs=[
            pl.BlockSpec((sources, small, features), lambda i: (0, large // small, 0)),
            pl.BlockSpec((per_step, large, features), lambda i: (i, 0, 0)),
            pl.BlockSpec(memory_space=pl.ANY),
            pl.BlockSpec(memory_space=pl.ANY),
            pl.BlockSpec(memory_space=pl.ANY),
        ],
        out_specs=(
            pl.BlockSpec((per_step, large, features), lambda i: (i, 0, 0)),
            pl.BlockSpec(memory_space=pl.ANY),
        ),
        scratch_shapes=[
            pltpu.VMEM((sources, small, features), received.dtype),
            pltpu.VMEM(gate_matrix.shape, gate_matrix.dtype),
            pltpu.VMEM(up_matrix.shape, up_matrix.dtype),
            pltpu.VMEM(down_matrix.shape, down_matrix.dtype),
            pltpu.SemaphoreType.DMA((n,)),
            pltpu.SemaphoreType.DMA((n,)),
            pltpu.SemaphoreType.DMA,
            pltpu.SemaphoreType.DMA((3,)),
        ],
        compiler_params=pltpu.CompilerParams(
            collective_id=0, has_side_effects=True, vmem_limit_bytes=60 * 1024 * 1024
        ),
        cost_estimate=pl.CostEstimate(
            flops=6 * sources * slot_bound * features * hidden,
            transcendentals=sources * slot_bound * hidden,
            bytes_accessed=2 * (2 * sources * slot_bound * features + 3 * features * hidden),
        ),
    )(received, received, gate_matrix, up_matrix, down_matrix)


def split_bf16(values):
    first = lax.reduce_precision(values, exponent_bits=8, mantissa_bits=7)
    second = values - first
    return tuple(part.astype(jnp.bfloat16) for part in (first, second))


def shards(tokens, expert_ids, gate_values, w_gate, w_up, w_down):
    token_count, features = tokens.shape
    topk_width = expert_ids.shape[1]
    local_count = w_gate.shape[0]
    experts_all = lax.axis_size("expert") * local_count
    other_bound = min(
        token_count,
        ((topk_width - 1) * token_count + experts_all - 3) // (experts_all - 2) * 3 // 2,
    )
    favoured_bound = token_count * 9 // 16
    slot_bound = max(favoured_bound, other_bound)
    buffer_rows = experts_all * slot_bound

    flat_ids = expert_ids.reshape(-1)
    one_hot = (flat_ids[:, None] == jnp.arange(experts_all, dtype=jnp.int32)[None, :]).astype(
        jnp.bfloat16
    )
    pair_count = flat_ids.shape[0]
    pair_index = jnp.arange(pair_count, dtype=jnp.int32)
    before = (pair_index[:, None] > pair_index[None, :]).astype(jnp.bfloat16)
    earlier = jnp.dot(before, one_hot, preferred_element_type=jnp.float32)
    slot_of = jnp.sum(earlier * one_hot.astype(jnp.float32), axis=1).astype(jnp.int32)
    places = (flat_ids * slot_bound + slot_of).reshape(token_count, topk_width)

    hit = (
        places[:, :, None] == jnp.arange(buffer_rows, dtype=jnp.int32)[None, None, :]
    ).reshape(token_count, topk_width, experts_all, slot_bound)
    pick = jnp.any(hit, axis=1).astype(jnp.bfloat16)
    outgoing = jnp.einsum(
        "tes,td->esd", pick, tokens, preferred_element_type=jnp.float32
    ).astype(jnp.bfloat16)
    received = lax.all_to_all(outgoing, "expert", split_axis=0, concat_axis=0, tiled=True)

    large = slot_bound - slot_bound // 9
    answered, returned_small = expert_blocks(received, w_gate[0], w_up[0], w_down[0], large, 8)
    returned_large = lax.all_to_all(answered, "expert", split_axis=0, concat_axis=0, tiled=True)
    weight_parts = split_bf16(gate_values)
    summed = None
    for begin, end, returned in ((large, slot_bound, returned_small), (0, large, returned_large)):
        stacked = jnp.stack(
            [
                jnp.sum(
                    jnp.where(
                        hit[:, :, :, begin:end], part.astype(jnp.float32)[:, :, None, None], 0.0
                    ),
                    axis=1,
                )
                for part in weight_parts
            ]
        ).astype(jnp.bfloat16)
        terms = jnp.einsum("ptes,esd->ptd", stacked, returned, preferred_element_type=jnp.float32)
        term = jnp.sum(terms, axis=0)
        summed = term if summed is None else summed + term
    return summed.astype(jnp.bfloat16)


def solution(mesh):
    placed = (
        P(("dp", "expert"), None),
        P(("dp", "expert"), None),
        P(("dp", "expert"), None),
        P("expert", None, None),
        P("expert", None, None),
        P("expert", None, None),
    )
    return jax.shard_map(
        shards, mesh=mesh, in_specs=placed, out_specs=P(("dp", "expert"), None), check_vma=False
    )
```

```python
import functools

import jax
import jax.numpy as jnp
from jax import lax
from jax.experimental import pallas as pl
from jax.experimental.pallas import tpu as pltpu
from jax.sharding import PartitionSpec as P

MESH = pl.DeviceIdType.MESH


def expert_apply(row_block, gate_matrix, up_matrix, down_matrix):
    gate_part = jnp.dot(row_block, gate_matrix, preferred_element_type=jnp.float32)
    up_part = jnp.dot(row_block, up_matrix, preferred_element_type=jnp.float32)
    hidden = (jax.nn.silu(gate_part) * up_part).astype(jnp.bfloat16)
    return jnp.dot(hidden, down_matrix, preferred_element_type=jnp.float32).astype(jnp.bfloat16)


def ffn_kernel(
    n, small_ref, large_ref, gate_hbm, up_hbm, down_hbm, large_out, small_out,
    held, gate_ref, up_ref, down_ref, send_sem, recv_sem, local_sem, weight_sem,
):
    step = pl.program_id(0)
    me = lax.axis_index("expert")
    local = pltpu.make_async_copy(held.at[me], small_out.at[me], local_sem)

    def remote(k):
        target = lax.rem(me + k, n)
        return pltpu.make_async_remote_copy(
            src_ref=held.at[target],
            dst_ref=small_out.at[me],
            send_sem=send_sem.at[k],
            recv_sem=recv_sem.at[k],
            device_id={"expert": target},
            device_id_type=MESH,
        )

    def start(k, carry):
        remote(k).start()
        return carry

    def finish(k, carry):
        remote(k).wait()
        return carry

    fetches = [
        pltpu.make_async_copy(source, target, weight_sem.at[index])
        for index, (source, target) in enumerate(
            ((gate_hbm, gate_ref), (up_hbm, up_ref), (down_hbm, down_ref))
        )
    ]

    @pl.when(step == 0)
    def _():
        for fetch in fetches:
            fetch.start()
        barrier = pltpu.get_barrier_semaphore()

        def greet(k, carry):
            pl.semaphore_signal(
                barrier, inc=1, device_id={"expert": lax.rem(me + k, n)}, device_id_type=MESH
            )
            return carry

        lax.fori_loop(1, n, greet, 0)
        pl.semaphore_wait(barrier, n - 1)
        sources, slots, features = small_ref.shape
        rows = small_ref[...].reshape(sources * slots, features)
        fetches[0].wait()
        gate_part = jnp.dot(rows, gate_ref[...], preferred_element_type=jnp.float32)
        fetches[1].wait()
        up_part = jnp.dot(rows, up_ref[...], preferred_element_type=jnp.float32)
        hidden = (jax.nn.silu(gate_part) * up_part).astype(jnp.bfloat16)
        fetches[2].wait()
        held[...] = (
            jnp.dot(hidden, down_ref[...], preferred_element_type=jnp.float32)
            .astype(jnp.bfloat16)
            .reshape(sources, slots, features)
        )
        local.start()
        lax.fori_loop(1, n, start, 0)

    sources, slots, features = large_ref.shape
    rows = large_ref[...].reshape(sources * slots, features)
    large_out[...] = expert_apply(rows, gate_ref[...], up_ref[...], down_ref[...]).reshape(
        sources, slots, features
    )

    @pl.when(step == pl.num_programs(0) - 1)
    def _():
        lax.fori_loop(1, n, finish, 0)
        local.wait()


def expert_blocks(received, gate_matrix, up_matrix, down_matrix, large, per_step):
    n = lax.axis_size("expert")
    sources, slot_bound, features = received.shape
    small = slot_bound - large
    hidden = gate_matrix.shape[1]
    return pl.pallas_call(
        functools.partial(ffn_kernel, n),
        out_shape=(
            jax.ShapeDtypeStruct((sources, large, features), received.dtype),
            jax.ShapeDtypeStruct((sources, small, features), received.dtype),
        ),
        grid=(sources // per_step,),
        in_specs=[
            pl.BlockSpec((sources, small, features), lambda i: (0, large // small, 0)),
            pl.BlockSpec((per_step, large, features), lambda i: (i, 0, 0)),
            pl.BlockSpec(memory_space=pl.ANY),
            pl.BlockSpec(memory_space=pl.ANY),
            pl.BlockSpec(memory_space=pl.ANY),
        ],
        out_specs=(
            pl.BlockSpec((per_step, large, features), lambda i: (i, 0, 0)),
            pl.BlockSpec(memory_space=pl.ANY),
        ),
        scratch_shapes=[
            pltpu.VMEM((sources, small, features), received.dtype),
            pltpu.VMEM(gate_matrix.shape, gate_matrix.dtype),
            pltpu.VMEM(up_matrix.shape, up_matrix.dtype),
            pltpu.VMEM(down_matrix.shape, down_matrix.dtype),
            pltpu.SemaphoreType.DMA((n,)),
            pltpu.SemaphoreType.DMA((n,)),
            pltpu.SemaphoreType.DMA,
            pltpu.SemaphoreType.DMA((3,)),
        ],
        compiler_params=pltpu.CompilerParams(
            collective_id=0, has_side_effects=True, vmem_limit_bytes=60 * 1024 * 1024
        ),
        cost_estimate=pl.CostEstimate(
            flops=6 * sources * slot_bound * features * hidden,
            transcendentals=sources * slot_bound * hidden,
            bytes_accessed=2 * (2 * sources * slot_bound * features + 3 * features * hidden),
        ),
    )(received, received, gate_matrix, up_matrix, down_matrix)


def split_bf16(values):
    first = lax.reduce_precision(values, exponent_bits=8, mantissa_bits=7)
    second = values - first
    return tuple(part.astype(jnp.bfloat16) for part in (first, second))


def shards(tokens, expert_ids, gate_values, w_gate, w_up, w_down):
    token_count, features = tokens.shape
    topk_width = expert_ids.shape[1]
    local_count = w_gate.shape[0]
    experts_all = lax.axis_size("expert") * local_count
    other_bound = min(
        token_count,
        ((topk_width - 1) * token_count + experts_all - 3) // (experts_all - 2) * 3 // 2,
    )
    favoured_bound = token_count * 9 // 16
    slot_bound = max(favoured_bound, other_bound)
    buffer_rows = experts_all * slot_bound

    flat_ids = expert_ids.reshape(-1)
    one_hot = (flat_ids[:, None] == jnp.arange(experts_all, dtype=jnp.int32)[None, :]).astype(
        jnp.bfloat16
    )
    pair_count = flat_ids.shape[0]
    pair_index = jnp.arange(pair_count, dtype=jnp.int32)
    before = (pair_index[:, None] > pair_index[None, :]).astype(jnp.bfloat16)
    earlier = jnp.dot(before, one_hot, preferred_element_type=jnp.float32)
    slot_of = jnp.sum(earlier * one_hot.astype(jnp.float32), axis=1).astype(jnp.int32)
    places = (flat_ids * slot_bound + slot_of).reshape(token_count, topk_width)

    hit = (
        places[:, :, None] == jnp.arange(buffer_rows, dtype=jnp.int32)[None, None, :]
    ).reshape(token_count, topk_width, experts_all, slot_bound)
    pick = jnp.any(hit, axis=1).astype(jnp.bfloat16)
    outgoing = jnp.einsum(
        "tes,td->esd", pick, tokens, preferred_element_type=jnp.float32
    ).astype(jnp.bfloat16)
    received = lax.all_to_all(outgoing, "expert", split_axis=0, concat_axis=0, tiled=True)

    large = slot_bound - slot_bound // 3
    answered, returned_small = expert_blocks(received, w_gate[0], w_up[0], w_down[0], large, 4)
    returned_large = lax.all_to_all(answered, "expert", split_axis=0, concat_axis=0, tiled=True)
    weight_parts = split_bf16(gate_values)
    summed = None
    for begin, end, returned in ((large, slot_bound, returned_small), (0, large, returned_large)):
        stacked = jnp.stack(
            [
                jnp.sum(
                    jnp.where(
                        hit[:, :, :, begin:end], part.astype(jnp.float32)[:, :, None, None], 0.0
                    ),
                    axis=1,
                )
                for part in weight_parts
            ]
        ).astype(jnp.bfloat16)
        terms = jnp.einsum("ptes,esd->ptd", stacked, returned, preferred_element_type=jnp.float32)
        term = jnp.sum(terms, axis=0)
        summed = term if summed is None else summed + term
    return summed.astype(jnp.bfloat16)


def solution(mesh):
    placed = (
        P(("dp", "expert"), None),
        P(("dp", "expert"), None),
        P(("dp", "expert"), None),
        P("expert", None, None),
        P("expert", None, None),
        P("expert", None, None),
    )
    return jax.shard_map(
        shards, mesh=mesh, in_specs=placed, out_specs=P(("dp", "expert"), None), check_vma=False
    )
```

```python
import functools

import jax
import jax.numpy as jnp
from jax import lax
from jax.experimental import pallas as pl
from jax.experimental.pallas import tpu as pltpu
from jax.sharding import PartitionSpec as P

MESH = pl.DeviceIdType.MESH


def expert_apply(row_block, gate_matrix, up_matrix, down_matrix):
    gate_part = jnp.dot(row_block, gate_matrix, preferred_element_type=jnp.float32)
    up_part = jnp.dot(row_block, up_matrix, preferred_element_type=jnp.float32)
    hidden = (jax.nn.silu(gate_part) * up_part).astype(jnp.bfloat16)
    return jnp.dot(hidden, down_matrix, preferred_element_type=jnp.float32).astype(jnp.bfloat16)


def ffn_kernel(
    n, small_ref, large_ref, gate_hbm, up_hbm, down_hbm, large_out, small_out,
    held, gate_ref, up_ref, down_ref, send_sem, recv_sem, local_sem, weight_sem,
):
    step = pl.program_id(0)
    me = lax.axis_index("expert")
    local = pltpu.make_async_copy(held.at[me], small_out.at[me], local_sem)

    def remote(k):
        target = lax.rem(me + k, n)
        return pltpu.make_async_remote_copy(
            src_ref=held.at[target],
            dst_ref=small_out.at[me],
            send_sem=send_sem.at[k],
            recv_sem=recv_sem.at[k],
            device_id={"expert": target},
            device_id_type=MESH,
        )

    def start(k, carry):
        remote(k).start()
        return carry

    def finish(k, carry):
        remote(k).wait()
        return carry

    fetches = [
        pltpu.make_async_copy(source, target, weight_sem.at[index])
        for index, (source, target) in enumerate(
            ((gate_hbm, gate_ref), (up_hbm, up_ref), (down_hbm, down_ref))
        )
    ]

    @pl.when(step == 0)
    def _():
        for fetch in fetches:
            fetch.start()
        sources, slots, features = small_ref.shape
        rows = small_ref[...].reshape(sources * slots, features)
        fetches[0].wait()
        gate_part = jnp.dot(rows, gate_ref[...], preferred_element_type=jnp.float32)
        fetches[1].wait()
        up_part = jnp.dot(rows, up_ref[...], preferred_element_type=jnp.float32)
        hidden = (jax.nn.silu(gate_part) * up_part).astype(jnp.bfloat16)
        fetches[2].wait()
        held[...] = (
            jnp.dot(hidden, down_ref[...], preferred_element_type=jnp.float32)
            .astype(jnp.bfloat16)
            .reshape(sources, slots, features)
        )
        local.start()
        barrier = pltpu.get_barrier_semaphore()

        def greet(k, carry):
            pl.semaphore_signal(
                barrier, inc=1, device_id={"expert": lax.rem(me + k, n)}, device_id_type=MESH
            )
            return carry

        lax.fori_loop(1, n, greet, 0)
        pl.semaphore_wait(barrier, n - 1)
        lax.fori_loop(1, n, start, 0)

    sources, slots, features = large_ref.shape
    rows = large_ref[...].reshape(sources * slots, features)
    large_out[...] = expert_apply(rows, gate_ref[...], up_ref[...], down_ref[...]).reshape(
        sources, slots, features
    )

    @pl.when(step == pl.num_programs(0) - 1)
    def _():
        lax.fori_loop(1, n, finish, 0)
        local.wait()


def expert_blocks(received, gate_matrix, up_matrix, down_matrix, large, per_step):
    n = lax.axis_size("expert")
    sources, slot_bound, features = received.shape
    small = slot_bound - large
    hidden = gate_matrix.shape[1]
    return pl.pallas_call(
        functools.partial(ffn_kernel, n),
        out_shape=(
            jax.ShapeDtypeStruct((sources, large, features), received.dtype),
            jax.ShapeDtypeStruct((sources, small, features), received.dtype),
        ),
        grid=(sources // per_step,),
        in_specs=[
            pl.BlockSpec((sources, small, features), lambda i: (0, large // small, 0)),
            pl.BlockSpec((per_step, large, features), lambda i: (i, 0, 0)),
            pl.BlockSpec(memory_space=pl.ANY),
            pl.BlockSpec(memory_space=pl.ANY),
            pl.BlockSpec(memory_space=pl.ANY),
        ],
        out_specs=(
            pl.BlockSpec((per_step, large, features), lambda i: (i, 0, 0)),
            pl.BlockSpec(memory_space=pl.ANY),
        ),
        scratch_shapes=[
            pltpu.VMEM((sources, small, features), received.dtype),
            pltpu.VMEM(gate_matrix.shape, gate_matrix.dtype),
            pltpu.VMEM(up_matrix.shape, up_matrix.dtype),
            pltpu.VMEM(down_matrix.shape, down_matrix.dtype),
            pltpu.SemaphoreType.DMA((n,)),
            pltpu.SemaphoreType.DMA((n,)),
            pltpu.SemaphoreType.DMA,
            pltpu.SemaphoreType.DMA((3,)),
        ],
        compiler_params=pltpu.CompilerParams(
            collective_id=0, has_side_effects=True, vmem_limit_bytes=60 * 1024 * 1024
        ),
        cost_estimate=pl.CostEstimate(
            flops=6 * sources * slot_bound * features * hidden,
            transcendentals=sources * slot_bound * hidden,
            bytes_accessed=2 * (2 * sources * slot_bound * features + 3 * features * hidden),
        ),
    )(received, received, gate_matrix, up_matrix, down_matrix)


def split_bf16(values):
    first = lax.reduce_precision(values, exponent_bits=8, mantissa_bits=7)
    second = values - first
    return tuple(part.astype(jnp.bfloat16) for part in (first, second))


def shards(tokens, expert_ids, gate_values, w_gate, w_up, w_down):
    token_count, features = tokens.shape
    topk_width = expert_ids.shape[1]
    local_count = w_gate.shape[0]
    experts_all = lax.axis_size("expert") * local_count
    other_bound = min(
        token_count,
        ((topk_width - 1) * token_count + experts_all - 3) // (experts_all - 2) * 3 // 2,
    )
    favoured_bound = token_count * 9 // 16
    slot_bound = max(favoured_bound, other_bound)
    buffer_rows = experts_all * slot_bound

    flat_ids = expert_ids.reshape(-1)
    one_hot = (flat_ids[:, None] == jnp.arange(experts_all, dtype=jnp.int32)[None, :]).astype(
        jnp.bfloat16
    )
    pair_count = flat_ids.shape[0]
    pair_index = jnp.arange(pair_count, dtype=jnp.int32)
    before = (pair_index[:, None] > pair_index[None, :]).astype(jnp.bfloat16)
    earlier = jnp.dot(before, one_hot, preferred_element_type=jnp.float32)
    slot_of = jnp.sum(earlier * one_hot.astype(jnp.float32), axis=1).astype(jnp.int32)
    places = (flat_ids * slot_bound + slot_of).reshape(token_count, topk_width)

    hit = (
        places[:, :, None] == jnp.arange(buffer_rows, dtype=jnp.int32)[None, None, :]
    ).reshape(token_count, topk_width, experts_all, slot_bound)
    pick = jnp.any(hit, axis=1).astype(jnp.bfloat16)
    outgoing = jnp.einsum(
        "tes,td->esd", pick, tokens, preferred_element_type=jnp.float32
    ).astype(jnp.bfloat16)
    received = lax.all_to_all(outgoing, "expert", split_axis=0, concat_axis=0, tiled=True)

    large = slot_bound - slot_bound // 9
    answered, returned_small = expert_blocks(received, w_gate[0], w_up[0], w_down[0], large, 4)
    returned_large = lax.all_to_all(answered, "expert", split_axis=0, concat_axis=0, tiled=True)
    weight_parts = split_bf16(gate_values)
    summed = None
    for begin, end, returned in ((large, slot_bound, returned_small), (0, large, returned_large)):
        stacked = jnp.stack(
            [
                jnp.sum(
                    jnp.where(
                        hit[:, :, :, begin:end], part.astype(jnp.float32)[:, :, None, None], 0.0
                    ),
                    axis=1,
                )
                for part in weight_parts
            ]
        ).astype(jnp.bfloat16)
        terms = jnp.einsum("ptes,esd->ptd", stacked, returned, preferred_element_type=jnp.float32)
        term = jnp.sum(terms, axis=0)
        summed = term if summed is None else summed + term
    return summed.astype(jnp.bfloat16)


def solution(mesh):
    placed = (
        P(("dp", "expert"), None),
        P(("dp", "expert"), None),
        P(("dp", "expert"), None),
        P("expert", None, None),
        P("expert", None, None),
        P("expert", None, None),
    )
    return jax.shard_map(
        shards, mesh=mesh, in_specs=placed, out_specs=P(("dp", "expert"), None), check_vma=False
    )
```

```python
import functools

import jax
import jax.numpy as jnp
from jax import lax
from jax.experimental import pallas as pl
from jax.experimental.pallas import tpu as pltpu
from jax.sharding import PartitionSpec as P

MESH = pl.DeviceIdType.MESH


def expert_apply(row_block, gate_matrix, up_matrix, down_matrix):
    gate_part = jnp.dot(row_block, gate_matrix, preferred_element_type=jnp.float32)
    up_part = jnp.dot(row_block, up_matrix, preferred_element_type=jnp.float32)
    hidden = (jax.nn.silu(gate_part) * up_part).astype(jnp.bfloat16)
    return jnp.dot(hidden, down_matrix, preferred_element_type=jnp.float32).astype(jnp.bfloat16)


def ffn_kernel(
    n, small_ref, large_ref, gate_hbm, up_hbm, down_hbm, large_out, small_out,
    held, gate_up_ref, down_ref, send_sem, recv_sem, local_sem, weight_sem,
):
    step = pl.program_id(0)
    me = lax.axis_index("expert")
    local = pltpu.make_async_copy(held.at[me], small_out.at[me], local_sem)

    def remote(k):
        target = lax.rem(me + k, n)
        return pltpu.make_async_remote_copy(
            src_ref=held.at[target],
            dst_ref=small_out.at[me],
            send_sem=send_sem.at[k],
            recv_sem=recv_sem.at[k],
            device_id={"expert": target},
            device_id_type=MESH,
        )

    def start(k, carry):
        remote(k).start()
        return carry

    def finish(k, carry):
        remote(k).wait()
        return carry

    hidden = down_ref.shape[0]
    fetches = [
        pltpu.make_async_copy(source, target, weight_sem.at[index])
        for index, (source, target) in enumerate(
            (
                (gate_hbm, gate_up_ref.at[:, pl.ds(0, hidden)]),
                (up_hbm, gate_up_ref.at[:, pl.ds(hidden, hidden)]),
                (down_hbm, down_ref),
            )
        )
    ]

    def apply(rows):
        both = jnp.dot(rows, gate_up_ref[...], preferred_element_type=jnp.float32)
        gate_part, up_part = both[:, :hidden], both[:, hidden:]
        mixed = (jax.nn.silu(gate_part) * up_part).astype(jnp.bfloat16)
        return jnp.dot(mixed, down_ref[...], preferred_element_type=jnp.float32).astype(
            jnp.bfloat16
        )

    @pl.when(step == 0)
    def _():
        for fetch in fetches:
            fetch.start()
        barrier = pltpu.get_barrier_semaphore()

        def greet(k, carry):
            pl.semaphore_signal(
                barrier, inc=1, device_id={"expert": lax.rem(me + k, n)}, device_id_type=MESH
            )
            return carry

        lax.fori_loop(1, n, greet, 0)
        pl.semaphore_wait(barrier, n - 1)
        sources, slots, features = small_ref.shape
        rows = small_ref[...].reshape(sources * slots, features)
        for fetch in fetches:
            fetch.wait()
        held[...] = apply(rows).reshape(sources, slots, features)
        local.start()
        lax.fori_loop(1, n, start, 0)

    sources, slots, features = large_ref.shape
    rows = large_ref[...].reshape(sources * slots, features)
    large_out[...] = apply(rows).reshape(sources, slots, features)

    @pl.when(step == pl.num_programs(0) - 1)
    def _():
        lax.fori_loop(1, n, finish, 0)
        local.wait()


def expert_blocks(received, gate_matrix, up_matrix, down_matrix, large, per_step):
    n = lax.axis_size("expert")
    sources, slot_bound, features = received.shape
    small = slot_bound - large
    hidden = gate_matrix.shape[1]
    return pl.pallas_call(
        functools.partial(ffn_kernel, n),
        out_shape=(
            jax.ShapeDtypeStruct((sources, large, features), received.dtype),
            jax.ShapeDtypeStruct((sources, small, features), received.dtype),
        ),
        grid=(sources // per_step,),
        in_specs=[
            pl.BlockSpec((sources, small, features), lambda i: (0, large // small, 0)),
            pl.BlockSpec((per_step, large, features), lambda i: (i, 0, 0)),
            pl.BlockSpec(memory_space=pl.ANY),
            pl.BlockSpec(memory_space=pl.ANY),
            pl.BlockSpec(memory_space=pl.ANY),
        ],
        out_specs=(
            pl.BlockSpec((per_step, large, features), lambda i: (i, 0, 0)),
            pl.BlockSpec(memory_space=pl.ANY),
        ),
        scratch_shapes=[
            pltpu.VMEM((sources, small, features), received.dtype),
            pltpu.VMEM((features, 2 * hidden), gate_matrix.dtype),
            pltpu.VMEM(down_matrix.shape, down_matrix.dtype),
            pltpu.SemaphoreType.DMA((n,)),
            pltpu.SemaphoreType.DMA((n,)),
            pltpu.SemaphoreType.DMA,
            pltpu.SemaphoreType.DMA((3,)),
        ],
        compiler_params=pltpu.CompilerParams(
            collective_id=0, has_side_effects=True, vmem_limit_bytes=60 * 1024 * 1024
        ),
        cost_estimate=pl.CostEstimate(
            flops=6 * sources * slot_bound * features * hidden,
            transcendentals=sources * slot_bound * hidden,
            bytes_accessed=2 * (2 * sources * slot_bound * features + 3 * features * hidden),
        ),
    )(received, received, gate_matrix, up_matrix, down_matrix)


def split_bf16(values):
    first = lax.reduce_precision(values, exponent_bits=8, mantissa_bits=7)
    second = values - first
    return tuple(part.astype(jnp.bfloat16) for part in (first, second))


def shards(tokens, expert_ids, gate_values, w_gate, w_up, w_down):
    token_count, features = tokens.shape
    topk_width = expert_ids.shape[1]
    local_count = w_gate.shape[0]
    experts_all = lax.axis_size("expert") * local_count
    other_bound = min(
        token_count,
        ((topk_width - 1) * token_count + experts_all - 3) // (experts_all - 2) * 3 // 2,
    )
    favoured_bound = token_count * 9 // 16
    slot_bound = max(favoured_bound, other_bound)
    buffer_rows = experts_all * slot_bound

    flat_ids = expert_ids.reshape(-1)
    one_hot = (flat_ids[:, None] == jnp.arange(experts_all, dtype=jnp.int32)[None, :]).astype(
        jnp.bfloat16
    )
    pair_count = flat_ids.shape[0]
    pair_index = jnp.arange(pair_count, dtype=jnp.int32)
    before = (pair_index[:, None] > pair_index[None, :]).astype(jnp.bfloat16)
    earlier = jnp.dot(before, one_hot, preferred_element_type=jnp.float32)
    slot_of = jnp.sum(earlier * one_hot.astype(jnp.float32), axis=1).astype(jnp.int32)
    places = (flat_ids * slot_bound + slot_of).reshape(token_count, topk_width)

    hit = (
        places[:, :, None] == jnp.arange(buffer_rows, dtype=jnp.int32)[None, None, :]
    ).reshape(token_count, topk_width, experts_all, slot_bound)
    pick = jnp.any(hit, axis=1).astype(jnp.bfloat16)
    outgoing = jnp.einsum(
        "tes,td->esd", pick, tokens, preferred_element_type=jnp.float32
    ).astype(jnp.bfloat16)
    received = lax.all_to_all(outgoing, "expert", split_axis=0, concat_axis=0, tiled=True)

    large = slot_bound - slot_bound // 9
    answered, returned_small = expert_blocks(received, w_gate[0], w_up[0], w_down[0], large, 4)
    returned_large = lax.all_to_all(answered, "expert", split_axis=0, concat_axis=0, tiled=True)
    weight_parts = split_bf16(gate_values)
    summed = None
    for begin, end, returned in ((large, slot_bound, returned_small), (0, large, returned_large)):
        stacked = jnp.stack(
            [
                jnp.sum(
                    jnp.where(
                        hit[:, :, :, begin:end], part.astype(jnp.float32)[:, :, None, None], 0.0
                    ),
                    axis=1,
                )
                for part in weight_parts
            ]
        ).astype(jnp.bfloat16)
        terms = jnp.einsum("ptes,esd->ptd", stacked, returned, preferred_element_type=jnp.float32)
        term = jnp.sum(terms, axis=0)
        summed = term if summed is None else summed + term
    return summed.astype(jnp.bfloat16)


def solution(mesh):
    placed = (
        P(("dp", "expert"), None),
        P(("dp", "expert"), None),
        P(("dp", "expert"), None),
        P("expert", None, None),
        P("expert", None, None),
        P("expert", None, None),
    )
    return jax.shard_map(
        shards, mesh=mesh, in_specs=placed, out_specs=P(("dp", "expert"), None), check_vma=False
    )
```

```python
import functools

import jax
import jax.numpy as jnp
from jax import lax
from jax.experimental import pallas as pl
from jax.experimental.pallas import tpu as pltpu
from jax.sharding import PartitionSpec as P

MESH = pl.DeviceIdType.MESH


def expert_apply(row_block, gate_matrix, up_matrix, down_matrix):
    gate_part = jnp.dot(row_block, gate_matrix, preferred_element_type=jnp.float32)
    up_part = jnp.dot(row_block, up_matrix, preferred_element_type=jnp.float32)
    hidden = (jax.nn.silu(gate_part) * up_part).astype(jnp.bfloat16)
    return jnp.dot(hidden, down_matrix, preferred_element_type=jnp.float32).astype(jnp.bfloat16)


def ffn_kernel(
    n, small_ref, large_ref, gate_hbm, up_hbm, down_hbm, large_out, small_out,
    held, gate_up_ref, down_ref, send_sem, recv_sem, local_sem, weight_sem,
):
    step = pl.program_id(0)
    me = lax.axis_index("expert")
    local = pltpu.make_async_copy(held.at[me], small_out.at[me], local_sem)

    def remote(k):
        target = lax.rem(me + k, n)
        return pltpu.make_async_remote_copy(
            src_ref=held.at[target],
            dst_ref=small_out.at[me],
            send_sem=send_sem.at[k],
            recv_sem=recv_sem.at[k],
            device_id={"expert": target},
            device_id_type=MESH,
        )

    def start(k, carry):
        remote(k).start()
        return carry

    def finish(k, carry):
        remote(k).wait()
        return carry

    hidden = down_ref.shape[0]
    fetches = [
        pltpu.make_async_copy(source, target, weight_sem.at[index])
        for index, (source, target) in enumerate(
            (
                (gate_hbm, gate_up_ref.at[:, pl.ds(0, hidden)]),
                (up_hbm, gate_up_ref.at[:, pl.ds(hidden, hidden)]),
                (down_hbm, down_ref),
            )
        )
    ]

    def apply(rows):
        both = jnp.dot(rows, gate_up_ref[...], preferred_element_type=jnp.float32)
        gate_part, up_part = both[:, :hidden], both[:, hidden:]
        mixed = (jax.nn.silu(gate_part) * up_part).astype(jnp.bfloat16)
        return jnp.dot(mixed, down_ref[...], preferred_element_type=jnp.float32).astype(
            jnp.bfloat16
        )

    @pl.when(step == 0)
    def _():
        for fetch in fetches:
            fetch.start()
        barrier = pltpu.get_barrier_semaphore()

        def greet(k, carry):
            pl.semaphore_signal(
                barrier, inc=1, device_id={"expert": lax.rem(me + k, n)}, device_id_type=MESH
            )
            return carry

        lax.fori_loop(1, n, greet, 0)
        pl.semaphore_wait(barrier, n - 1)
        sources, slots, features = small_ref.shape
        rows = small_ref[...].reshape(sources * slots, features)
        for fetch in fetches:
            fetch.wait()
        held[...] = apply(rows).reshape(sources, slots, features)
        local.start()
        lax.fori_loop(1, n, start, 0)

    sources, slots, features = large_ref.shape
    rows = large_ref[...].reshape(sources * slots, features)
    large_out[...] = apply(rows).reshape(sources, slots, features)

    @pl.when(step == pl.num_programs(0) - 1)
    def _():
        lax.fori_loop(1, n, finish, 0)
        local.wait()


def expert_blocks(received, gate_matrix, up_matrix, down_matrix, large, per_step):
    n = lax.axis_size("expert")
    sources, slot_bound, features = received.shape
    small = slot_bound - large
    hidden = gate_matrix.shape[1]
    return pl.pallas_call(
        functools.partial(ffn_kernel, n),
        out_shape=(
            jax.ShapeDtypeStruct((sources, large, features), received.dtype),
            jax.ShapeDtypeStruct((sources, small, features), received.dtype),
        ),
        grid=(sources // per_step,),
        in_specs=[
            pl.BlockSpec((sources, small, features), lambda i: (0, large // small, 0)),
            pl.BlockSpec((per_step, large, features), lambda i: (i, 0, 0)),
            pl.BlockSpec(memory_space=pl.ANY),
            pl.BlockSpec(memory_space=pl.ANY),
            pl.BlockSpec(memory_space=pl.ANY),
        ],
        out_specs=(
            pl.BlockSpec((per_step, large, features), lambda i: (i, 0, 0)),
            pl.BlockSpec(memory_space=pl.ANY),
        ),
        scratch_shapes=[
            pltpu.VMEM((sources, small, features), received.dtype),
            pltpu.VMEM((features, 2 * hidden), gate_matrix.dtype),
            pltpu.VMEM(down_matrix.shape, down_matrix.dtype),
            pltpu.SemaphoreType.DMA((n,)),
            pltpu.SemaphoreType.DMA((n,)),
            pltpu.SemaphoreType.DMA,
            pltpu.SemaphoreType.DMA((3,)),
        ],
        compiler_params=pltpu.CompilerParams(
            collective_id=0, has_side_effects=True, vmem_limit_bytes=60 * 1024 * 1024
        ),
        cost_estimate=pl.CostEstimate(
            flops=6 * sources * slot_bound * features * hidden,
            transcendentals=sources * slot_bound * hidden,
            bytes_accessed=2 * (2 * sources * slot_bound * features + 3 * features * hidden),
        ),
    )(received, received, gate_matrix, up_matrix, down_matrix)


def split_bf16(values):
    first = lax.reduce_precision(values, exponent_bits=8, mantissa_bits=7)
    second = values - first
    return tuple(part.astype(jnp.bfloat16) for part in (first, second))


def shards(tokens, expert_ids, gate_values, w_gate, w_up, w_down):
    token_count, features = tokens.shape
    topk_width = expert_ids.shape[1]
    local_count = w_gate.shape[0]
    experts_all = lax.axis_size("expert") * local_count
    other_bound = min(
        token_count,
        ((topk_width - 1) * token_count + experts_all - 3) // (experts_all - 2) * 3 // 2,
    )
    favoured_bound = token_count * 9 // 16
    slot_bound = max(favoured_bound, other_bound)
    buffer_rows = experts_all * slot_bound

    flat_ids = expert_ids.reshape(-1)
    one_hot = (flat_ids[:, None] == jnp.arange(experts_all, dtype=jnp.int32)[None, :]).astype(
        jnp.bfloat16
    )
    pair_count = flat_ids.shape[0]
    pair_index = jnp.arange(pair_count, dtype=jnp.int32)
    before = (pair_index[:, None] > pair_index[None, :]).astype(jnp.bfloat16)
    earlier = jnp.dot(before, one_hot, preferred_element_type=jnp.float32)
    slot_of = jnp.sum(earlier * one_hot.astype(jnp.float32), axis=1).astype(jnp.int32)
    places = (flat_ids * slot_bound + slot_of).reshape(token_count, topk_width)

    hit = (
        places[:, :, None] == jnp.arange(buffer_rows, dtype=jnp.int32)[None, None, :]
    ).reshape(token_count, topk_width, experts_all, slot_bound)
    pick = jnp.any(hit, axis=1).astype(jnp.bfloat16)
    outgoing = jnp.einsum(
        "tes,td->esd", pick, tokens, preferred_element_type=jnp.float32
    ).astype(jnp.bfloat16)
    received = lax.all_to_all(outgoing, "expert", split_axis=0, concat_axis=0, tiled=True)

    large = slot_bound - slot_bound // 9
    answered, returned_small = expert_blocks(received, w_gate[0], w_up[0], w_down[0], large, 4)
    returned_large = lax.all_to_all(answered, "expert", split_axis=0, concat_axis=0, tiled=True)
    weight_parts = split_bf16(gate_values)
    experts = jnp.arange(experts_all, dtype=jnp.int32)
    slots = slot_of.reshape(token_count, topk_width)
    summed = None
    for begin, end, returned in ((large, slot_bound, returned_small), (0, large, returned_large)):
        stacked = jnp.stack(
            [
                jnp.sum(
                    jnp.where(
                        (expert_ids[:, :, None, None] == experts[None, None, :, None])
                        & (slots[:, :, None, None] == jnp.arange(begin, end)[None, None, None, :]),
                        part.astype(jnp.float32)[:, :, None, None],
                        0.0,
                    ),
                    axis=1,
                )
                for part in weight_parts
            ]
        ).astype(jnp.bfloat16)
        terms = jnp.einsum("ptes,esd->ptd", stacked, returned, preferred_element_type=jnp.float32)
        term = jnp.sum(terms, axis=0)
        summed = term if summed is None else summed + term
    return summed.astype(jnp.bfloat16)


def solution(mesh):
    placed = (
        P(("dp", "expert"), None),
        P(("dp", "expert"), None),
        P(("dp", "expert"), None),
        P("expert", None, None),
        P("expert", None, None),
        P("expert", None, None),
    )
    return jax.shard_map(
        shards, mesh=mesh, in_specs=placed, out_specs=P(("dp", "expert"), None), check_vma=False
    )
```

```python
import functools

import jax
import jax.numpy as jnp
from jax import lax
from jax.experimental import pallas as pl
from jax.experimental.pallas import tpu as pltpu
from jax.sharding import PartitionSpec as P

MESH = pl.DeviceIdType.MESH


def expert_apply(row_block, gate_matrix, up_matrix, down_matrix):
    gate_part = jnp.dot(row_block, gate_matrix, preferred_element_type=jnp.float32)
    up_part = jnp.dot(row_block, up_matrix, preferred_element_type=jnp.float32)
    hidden = (jax.nn.silu(gate_part) * up_part).astype(jnp.bfloat16)
    return jnp.dot(hidden, down_matrix, preferred_element_type=jnp.float32).astype(jnp.bfloat16)


def ffn_kernel(
    n, small_ref, large_ref, gate_hbm, up_hbm, down_hbm, large_out, small_out,
    held, gate_up_ref, down_ref, send_sem, recv_sem, local_sem, weight_sem,
):
    step = pl.program_id(0)
    me = lax.axis_index("expert")
    local = pltpu.make_async_copy(held.at[me], small_out.at[me], local_sem)

    def remote(k):
        target = lax.rem(me + k, n)
        return pltpu.make_async_remote_copy(
            src_ref=held.at[target],
            dst_ref=small_out.at[me],
            send_sem=send_sem.at[k],
            recv_sem=recv_sem.at[k],
            device_id={"expert": target},
            device_id_type=MESH,
        )

    def start(k, carry):
        remote(k).start()
        return carry

    def finish(k, carry):
        remote(k).wait()
        return carry

    hidden = down_ref.shape[0]
    fetches = [
        pltpu.make_async_copy(source, target, weight_sem.at[index])
        for index, (source, target) in enumerate(
            (
                (gate_hbm, gate_up_ref.at[:, pl.ds(0, hidden)]),
                (up_hbm, gate_up_ref.at[:, pl.ds(hidden, hidden)]),
                (down_hbm, down_ref),
            )
        )
    ]

    def apply(rows):
        both = jnp.dot(rows, gate_up_ref[...], preferred_element_type=jnp.float32)
        gate_part, up_part = both[:, :hidden], both[:, hidden:]
        mixed = (jax.nn.silu(gate_part) * up_part).astype(jnp.bfloat16)
        return jnp.dot(mixed, down_ref[...], preferred_element_type=jnp.float32).astype(
            jnp.bfloat16
        )

    @pl.when(step == 0)
    def _():
        for fetch in fetches:
            fetch.start()
        barrier = pltpu.get_barrier_semaphore()

        def greet(k, carry):
            pl.semaphore_signal(
                barrier, inc=1, device_id={"expert": lax.rem(me + k, n)}, device_id_type=MESH
            )
            return carry

        lax.fori_loop(1, n, greet, 0)
        pl.semaphore_wait(barrier, n - 1)
        sources, slots, features = small_ref.shape
        rows = small_ref[...].reshape(sources * slots, features)
        for fetch in fetches:
            fetch.wait()
        held[...] = apply(rows).reshape(sources, slots, features)
        local.start()
        lax.fori_loop(1, n, start, 0)

    sources, slots, features = large_ref.shape
    rows = large_ref[...].reshape(sources * slots, features)
    large_out[...] = apply(rows).reshape(sources, slots, features)

    @pl.when(step == pl.num_programs(0) - 1)
    def _():
        lax.fori_loop(1, n, finish, 0)
        local.wait()


def expert_blocks(received, gate_matrix, up_matrix, down_matrix, large, per_step):
    n = lax.axis_size("expert")
    sources, slot_bound, features = received.shape
    small = slot_bound - large
    hidden = gate_matrix.shape[1]
    return pl.pallas_call(
        functools.partial(ffn_kernel, n),
        out_shape=(
            jax.ShapeDtypeStruct((sources, large, features), received.dtype),
            jax.ShapeDtypeStruct((sources, small, features), received.dtype),
        ),
        grid=(sources // per_step,),
        in_specs=[
            pl.BlockSpec((sources, small, features), lambda i: (0, large // small, 0)),
            pl.BlockSpec((per_step, large, features), lambda i: (i, 0, 0)),
            pl.BlockSpec(memory_space=pl.ANY),
            pl.BlockSpec(memory_space=pl.ANY),
            pl.BlockSpec(memory_space=pl.ANY),
        ],
        out_specs=(
            pl.BlockSpec((per_step, large, features), lambda i: (i, 0, 0)),
            pl.BlockSpec(memory_space=pl.ANY),
        ),
        scratch_shapes=[
            pltpu.VMEM((sources, small, features), received.dtype),
            pltpu.VMEM((features, 2 * hidden), gate_matrix.dtype),
            pltpu.VMEM(down_matrix.shape, down_matrix.dtype),
            pltpu.SemaphoreType.DMA((n,)),
            pltpu.SemaphoreType.DMA((n,)),
            pltpu.SemaphoreType.DMA,
            pltpu.SemaphoreType.DMA((3,)),
        ],
        compiler_params=pltpu.CompilerParams(
            collective_id=0, has_side_effects=True, vmem_limit_bytes=60 * 1024 * 1024
        ),
        cost_estimate=pl.CostEstimate(
            flops=6 * sources * slot_bound * features * hidden,
            transcendentals=sources * slot_bound * hidden,
            bytes_accessed=2 * (2 * sources * slot_bound * features + 3 * features * hidden),
        ),
    )(received, received, gate_matrix, up_matrix, down_matrix)


def split_bf16(values):
    first = lax.reduce_precision(values, exponent_bits=8, mantissa_bits=7)
    second = values - first
    return tuple(part.astype(jnp.bfloat16) for part in (first, second))


def shards(tokens, expert_ids, gate_values, w_gate, w_up, w_down):
    token_count, features = tokens.shape
    topk_width = expert_ids.shape[1]
    local_count = w_gate.shape[0]
    experts_all = lax.axis_size("expert") * local_count
    other_bound = min(
        token_count,
        ((topk_width - 1) * token_count + experts_all - 3) // (experts_all - 2) * 3 // 2,
    )
    favoured_bound = token_count * 9 // 16
    slot_bound = max(favoured_bound, other_bound)
    buffer_rows = experts_all * slot_bound

    flat_ids = expert_ids.T.reshape(-1)
    one_hot = (flat_ids[:, None] == jnp.arange(experts_all, dtype=jnp.int32)[None, :]).astype(
        jnp.bfloat16
    )
    pair_count = flat_ids.shape[0]
    pair_index = jnp.arange(pair_count, dtype=jnp.int32)
    before = (pair_index[:, None] > pair_index[None, :]).astype(jnp.bfloat16)
    earlier = jnp.dot(before, one_hot, preferred_element_type=jnp.float32)
    slot_of = jnp.sum(earlier * one_hot.astype(jnp.float32), axis=1).astype(jnp.int32)
    places = (flat_ids * slot_bound + slot_of).reshape(topk_width, token_count).T
    slot_of = slot_of.reshape(topk_width, token_count).T

    hit = (
        places[:, :, None] == jnp.arange(buffer_rows, dtype=jnp.int32)[None, None, :]
    ).reshape(token_count, topk_width, experts_all, slot_bound)
    pick = jnp.any(hit, axis=1).astype(jnp.bfloat16)
    outgoing = jnp.einsum(
        "tes,td->esd", pick, tokens, preferred_element_type=jnp.float32
    ).astype(jnp.bfloat16)
    received = lax.all_to_all(outgoing, "expert", split_axis=0, concat_axis=0, tiled=True)

    large = slot_bound - slot_bound // 9
    answered, returned_small = expert_blocks(received, w_gate[0], w_up[0], w_down[0], large, 4)
    returned_large = lax.all_to_all(answered, "expert", split_axis=0, concat_axis=0, tiled=True)
    weight_parts = split_bf16(gate_values)
    experts = jnp.arange(experts_all, dtype=jnp.int32)
    slots = slot_of
    summed = None
    for begin, end, returned in ((large, slot_bound, returned_small), (0, large, returned_large)):
        stacked = jnp.stack(
            [
                jnp.sum(
                    jnp.where(
                        (expert_ids[:, :, None, None] == experts[None, None, :, None])
                        & (slots[:, :, None, None] == jnp.arange(begin, end)[None, None, None, :]),
                        part.astype(jnp.float32)[:, :, None, None],
                        0.0,
                    ),
                    axis=1,
                )
                for part in weight_parts
            ]
        ).astype(jnp.bfloat16)
        terms = jnp.einsum("ptes,esd->ptd", stacked, returned, preferred_element_type=jnp.float32)
        term = jnp.sum(terms, axis=0)
        summed = term if summed is None else summed + term
    return summed.astype(jnp.bfloat16)


def solution(mesh):
    placed = (
        P(("dp", "expert"), None),
        P(("dp", "expert"), None),
        P(("dp", "expert"), None),
        P("expert", None, None),
        P("expert", None, None),
        P("expert", None, None),
    )
    return jax.shard_map(
        shards, mesh=mesh, in_specs=placed, out_specs=P(("dp", "expert"), None), check_vma=False
    )
```

```python
import functools

import jax
import jax.numpy as jnp
from jax import lax
from jax.experimental import pallas as pl
from jax.experimental.pallas import tpu as pltpu
from jax.sharding import PartitionSpec as P

MESH = pl.DeviceIdType.MESH


def expert_apply(row_block, gate_matrix, up_matrix, down_matrix):
    gate_part = jnp.dot(row_block, gate_matrix, preferred_element_type=jnp.float32)
    up_part = jnp.dot(row_block, up_matrix, preferred_element_type=jnp.float32)
    hidden = (jax.nn.silu(gate_part) * up_part).astype(jnp.bfloat16)
    return jnp.dot(hidden, down_matrix, preferred_element_type=jnp.float32).astype(jnp.bfloat16)


def ffn_kernel(
    n, small_ref, large_ref, gate_hbm, up_hbm, down_hbm, large_out, small_out,
    held, gate_up_ref, down_ref, send_sem, recv_sem, local_sem, weight_sem,
):
    step = pl.program_id(0)
    me = lax.axis_index("expert")
    local = pltpu.make_async_copy(held.at[me], small_out.at[me], local_sem)

    def remote(k):
        target = lax.rem(me + k, n)
        return pltpu.make_async_remote_copy(
            src_ref=held.at[target],
            dst_ref=small_out.at[me],
            send_sem=send_sem.at[k],
            recv_sem=recv_sem.at[k],
            device_id={"expert": target},
            device_id_type=MESH,
        )

    def start(k, carry):
        remote(k).start()
        return carry

    def finish(k, carry):
        remote(k).wait()
        return carry

    hidden = down_ref.shape[0]
    fetches = [
        pltpu.make_async_copy(source, target, weight_sem.at[index])
        for index, (source, target) in enumerate(
            (
                (gate_hbm, gate_up_ref.at[:, pl.ds(0, hidden)]),
                (up_hbm, gate_up_ref.at[:, pl.ds(hidden, hidden)]),
                (down_hbm, down_ref),
            )
        )
    ]

    def apply(rows):
        both = jnp.dot(rows, gate_up_ref[...], preferred_element_type=jnp.float32)
        gate_part, up_part = both[:, :hidden], both[:, hidden:]
        mixed = (jax.nn.silu(gate_part) * up_part).astype(jnp.bfloat16)
        return jnp.dot(mixed, down_ref[...], preferred_element_type=jnp.float32).astype(
            jnp.bfloat16
        )

    @pl.when(step == 0)
    def _():
        for fetch in fetches:
            fetch.start()
        barrier = pltpu.get_barrier_semaphore()

        def greet(k, carry):
            pl.semaphore_signal(
                barrier, inc=1, device_id={"expert": lax.rem(me + k, n)}, device_id_type=MESH
            )
            return carry

        lax.fori_loop(1, n, greet, 0)
        pl.semaphore_wait(barrier, n - 1)
        sources, slots, features = small_ref.shape
        rows = small_ref[...].reshape(sources * slots, features)
        for fetch in fetches:
            fetch.wait()
        held[...] = apply(rows).reshape(sources, slots, features)
        local.start()
        lax.fori_loop(1, n, start, 0)

    sources, slots, features = large_ref.shape
    rows = large_ref[...].reshape(sources * slots, features)
    large_out[...] = apply(rows).reshape(sources, slots, features)

    @pl.when(step == pl.num_programs(0) - 1)
    def _():
        lax.fori_loop(1, n, finish, 0)
        local.wait()


def expert_blocks(received, gate_matrix, up_matrix, down_matrix, large, per_step):
    n = lax.axis_size("expert")
    sources, slot_bound, features = received.shape
    small = slot_bound - large
    hidden = gate_matrix.shape[1]
    return pl.pallas_call(
        functools.partial(ffn_kernel, n),
        out_shape=(
            jax.ShapeDtypeStruct((sources, large, features), received.dtype),
            jax.ShapeDtypeStruct((sources, small, features), received.dtype),
        ),
        grid=(sources // per_step,),
        in_specs=[
            pl.BlockSpec((sources, small, features), lambda i: (0, large // small, 0)),
            pl.BlockSpec((per_step, large, features), lambda i: (i, 0, 0)),
            pl.BlockSpec(memory_space=pl.ANY),
            pl.BlockSpec(memory_space=pl.ANY),
            pl.BlockSpec(memory_space=pl.ANY),
        ],
        out_specs=(
            pl.BlockSpec((per_step, large, features), lambda i: (i, 0, 0)),
            pl.BlockSpec(memory_space=pl.ANY),
        ),
        scratch_shapes=[
            pltpu.VMEM((sources, small, features), received.dtype),
            pltpu.VMEM((features, 2 * hidden), gate_matrix.dtype),
            pltpu.VMEM(down_matrix.shape, down_matrix.dtype),
            pltpu.SemaphoreType.DMA((n,)),
            pltpu.SemaphoreType.DMA((n,)),
            pltpu.SemaphoreType.DMA,
            pltpu.SemaphoreType.DMA((3,)),
        ],
        compiler_params=pltpu.CompilerParams(
            collective_id=0, has_side_effects=True, vmem_limit_bytes=60 * 1024 * 1024
        ),
        cost_estimate=pl.CostEstimate(
            flops=6 * sources * slot_bound * features * hidden,
            transcendentals=sources * slot_bound * hidden,
            bytes_accessed=2 * (2 * sources * slot_bound * features + 3 * features * hidden),
        ),
    )(received, received, gate_matrix, up_matrix, down_matrix)


def split_bf16(values):
    first = lax.reduce_precision(values, exponent_bits=8, mantissa_bits=7)
    second = values - first
    return tuple(part.astype(jnp.bfloat16) for part in (first, second))


def shards(tokens, expert_ids, gate_values, w_gate, w_up, w_down):
    token_count, features = tokens.shape
    topk_width = expert_ids.shape[1]
    local_count = w_gate.shape[0]
    experts_all = lax.axis_size("expert") * local_count
    other_bound = min(
        token_count,
        ((topk_width - 1) * token_count + experts_all - 3) // (experts_all - 2) * 3 // 2,
    )
    favoured_bound = token_count * 9 // 16
    slot_bound = max(favoured_bound, other_bound)
    buffer_rows = experts_all * slot_bound

    flat_ids = expert_ids.T.reshape(-1)
    one_hot = (flat_ids[:, None] == jnp.arange(experts_all, dtype=jnp.int32)[None, :]).astype(
        jnp.bfloat16
    )
    pair_count = flat_ids.shape[0]
    pair_index = jnp.arange(pair_count, dtype=jnp.int32)
    before = (pair_index[:, None] > pair_index[None, :]).astype(jnp.bfloat16)
    earlier = jnp.dot(before, one_hot, preferred_element_type=jnp.float32)
    slot_of = jnp.sum(earlier * one_hot.astype(jnp.float32), axis=1).astype(jnp.int32)
    places = (flat_ids * slot_bound + slot_of).reshape(topk_width, token_count).T
    slot_of = slot_of.reshape(topk_width, token_count).T

    hit = (
        places[:, :, None] == jnp.arange(buffer_rows, dtype=jnp.int32)[None, None, :]
    ).reshape(token_count, topk_width, experts_all, slot_bound)
    pick = jnp.any(hit, axis=1).astype(jnp.bfloat16)
    outgoing = jnp.einsum(
        "tes,td->esd", pick, tokens, preferred_element_type=jnp.float32
    ).astype(jnp.bfloat16)
    received = lax.all_to_all(outgoing, "expert", split_axis=0, concat_axis=0, tiled=True)

    large = slot_bound - slot_bound // 9
    answered, returned_small = expert_blocks(received, w_gate[0], w_up[0], w_down[0], large, 8)
    returned_large = lax.all_to_all(answered, "expert", split_axis=0, concat_axis=0, tiled=True)
    weight_parts = split_bf16(gate_values)
    experts = jnp.arange(experts_all, dtype=jnp.int32)
    slots = slot_of
    summed = None
    for begin, end, returned in ((large, slot_bound, returned_small), (0, large, returned_large)):
        stacked = jnp.stack(
            [
                jnp.sum(
                    jnp.where(
                        (expert_ids[:, :, None, None] == experts[None, None, :, None])
                        & (slots[:, :, None, None] == jnp.arange(begin, end)[None, None, None, :]),
                        part.astype(jnp.float32)[:, :, None, None],
                        0.0,
                    ),
                    axis=1,
                )
                for part in weight_parts
            ]
        ).astype(jnp.bfloat16)
        terms = jnp.einsum("ptes,esd->ptd", stacked, returned, preferred_element_type=jnp.float32)
        term = jnp.sum(terms, axis=0)
        summed = term if summed is None else summed + term
    return summed.astype(jnp.bfloat16)


def solution(mesh):
    placed = (
        P(("dp", "expert"), None),
        P(("dp", "expert"), None),
        P(("dp", "expert"), None),
        P("expert", None, None),
        P("expert", None, None),
        P("expert", None, None),
    )
    return jax.shard_map(
        shards, mesh=mesh, in_specs=placed, out_specs=P(("dp", "expert"), None), check_vma=False
    )
```

```python
import functools

import jax
import jax.numpy as jnp
from jax import lax
from jax.experimental import pallas as pl
from jax.experimental.pallas import tpu as pltpu
from jax.sharding import PartitionSpec as P

MESH = pl.DeviceIdType.MESH


def expert_apply(row_block, gate_matrix, up_matrix, down_matrix):
    gate_part = jnp.dot(row_block, gate_matrix, preferred_element_type=jnp.float32)
    up_part = jnp.dot(row_block, up_matrix, preferred_element_type=jnp.float32)
    hidden = (jax.nn.silu(gate_part) * up_part).astype(jnp.bfloat16)
    return jnp.dot(hidden, down_matrix, preferred_element_type=jnp.float32).astype(jnp.bfloat16)


def ffn_kernel(
    n, small_ref, large_ref, gate_hbm, up_hbm, down_hbm, large_out, small_out,
    held, gate_up_ref, down_ref, send_sem, recv_sem, local_sem, weight_sem,
):
    step = pl.program_id(0)
    me = lax.axis_index("expert")
    local = pltpu.make_async_copy(held.at[me], small_out.at[me], local_sem)

    def remote(k):
        target = lax.rem(me + k, n)
        return pltpu.make_async_remote_copy(
            src_ref=held.at[target],
            dst_ref=small_out.at[me],
            send_sem=send_sem.at[k],
            recv_sem=recv_sem.at[k],
            device_id={"expert": target},
            device_id_type=MESH,
        )

    def start(k, carry):
        remote(k).start()
        return carry

    def finish(k, carry):
        remote(k).wait()
        return carry

    hidden = down_ref.shape[0]
    fetches = [
        pltpu.make_async_copy(source, target, weight_sem.at[index])
        for index, (source, target) in enumerate(
            (
                (gate_hbm, gate_up_ref.at[:, pl.ds(0, hidden)]),
                (up_hbm, gate_up_ref.at[:, pl.ds(hidden, hidden)]),
                (down_hbm, down_ref),
            )
        )
    ]

    def apply(rows, before_down=lambda: None):
        both = jnp.dot(rows, gate_up_ref[...], preferred_element_type=jnp.float32)
        gate_part, up_part = both[:, :hidden], both[:, hidden:]
        mixed = (jax.nn.silu(gate_part) * up_part).astype(jnp.bfloat16)
        before_down()
        return jnp.dot(mixed, down_ref[...], preferred_element_type=jnp.float32).astype(
            jnp.bfloat16
        )

    @pl.when(step == 0)
    def _():
        for fetch in fetches:
            fetch.start()
        barrier = pltpu.get_barrier_semaphore()

        def greet(k, carry):
            pl.semaphore_signal(
                barrier, inc=1, device_id={"expert": lax.rem(me + k, n)}, device_id_type=MESH
            )
            return carry

        lax.fori_loop(1, n, greet, 0)
        pl.semaphore_wait(barrier, n - 1)
        sources, slots, features = small_ref.shape
        rows = small_ref[...].reshape(sources * slots, features)
        fetches[0].wait()
        fetches[1].wait()
        held[...] = apply(rows, fetches[2].wait).reshape(sources, slots, features)
        local.start()
        lax.fori_loop(1, n, start, 0)

    sources, slots, features = large_ref.shape
    rows = large_ref[...].reshape(sources * slots, features)
    large_out[...] = apply(rows).reshape(sources, slots, features)

    @pl.when(step == pl.num_programs(0) - 1)
    def _():
        lax.fori_loop(1, n, finish, 0)
        local.wait()


def expert_blocks(received, gate_matrix, up_matrix, down_matrix, large, per_step):
    n = lax.axis_size("expert")
    sources, slot_bound, features = received.shape
    small = slot_bound - large
    hidden = gate_matrix.shape[1]
    return pl.pallas_call(
        functools.partial(ffn_kernel, n),
        out_shape=(
            jax.ShapeDtypeStruct((sources, large, features), received.dtype),
            jax.ShapeDtypeStruct((sources, small, features), received.dtype),
        ),
        grid=(sources // per_step,),
        in_specs=[
            pl.BlockSpec((sources, small, features), lambda i: (0, large // small, 0)),
            pl.BlockSpec((per_step, large, features), lambda i: (i, 0, 0)),
            pl.BlockSpec(memory_space=pl.ANY),
            pl.BlockSpec(memory_space=pl.ANY),
            pl.BlockSpec(memory_space=pl.ANY),
        ],
        out_specs=(
            pl.BlockSpec((per_step, large, features), lambda i: (i, 0, 0)),
            pl.BlockSpec(memory_space=pl.ANY),
        ),
        scratch_shapes=[
            pltpu.VMEM((sources, small, features), received.dtype),
            pltpu.VMEM((features, 2 * hidden), gate_matrix.dtype),
            pltpu.VMEM(down_matrix.shape, down_matrix.dtype),
            pltpu.SemaphoreType.DMA((n,)),
            pltpu.SemaphoreType.DMA((n,)),
            pltpu.SemaphoreType.DMA,
            pltpu.SemaphoreType.DMA((3,)),
        ],
        compiler_params=pltpu.CompilerParams(
            collective_id=0, has_side_effects=True, vmem_limit_bytes=60 * 1024 * 1024
        ),
        cost_estimate=pl.CostEstimate(
            flops=6 * sources * slot_bound * features * hidden,
            transcendentals=sources * slot_bound * hidden,
            bytes_accessed=2 * (2 * sources * slot_bound * features + 3 * features * hidden),
        ),
    )(received, received, gate_matrix, up_matrix, down_matrix)


def split_bf16(values):
    first = lax.reduce_precision(values, exponent_bits=8, mantissa_bits=7)
    second = values - first
    return tuple(part.astype(jnp.bfloat16) for part in (first, second))


def shards(tokens, expert_ids, gate_values, w_gate, w_up, w_down):
    token_count, features = tokens.shape
    topk_width = expert_ids.shape[1]
    local_count = w_gate.shape[0]
    experts_all = lax.axis_size("expert") * local_count
    other_bound = min(
        token_count,
        ((topk_width - 1) * token_count + experts_all - 3) // (experts_all - 2) * 3 // 2,
    )
    favoured_bound = token_count * 9 // 16
    slot_bound = max(favoured_bound, other_bound)
    buffer_rows = experts_all * slot_bound

    flat_ids = expert_ids.T.reshape(-1)
    one_hot = (flat_ids[:, None] == jnp.arange(experts_all, dtype=jnp.int32)[None, :]).astype(
        jnp.bfloat16
    )
    pair_count = flat_ids.shape[0]
    pair_index = jnp.arange(pair_count, dtype=jnp.int32)
    before = (pair_index[:, None] > pair_index[None, :]).astype(jnp.bfloat16)
    earlier = jnp.dot(before, one_hot, preferred_element_type=jnp.float32)
    slot_of = jnp.sum(earlier * one_hot.astype(jnp.float32), axis=1).astype(jnp.int32)
    places = (flat_ids * slot_bound + slot_of).reshape(topk_width, token_count).T
    slot_of = slot_of.reshape(topk_width, token_count).T

    hit = (
        places[:, :, None] == jnp.arange(buffer_rows, dtype=jnp.int32)[None, None, :]
    ).reshape(token_count, topk_width, experts_all, slot_bound)
    pick = jnp.any(hit, axis=1).astype(jnp.bfloat16)
    outgoing = jnp.einsum(
        "tes,td->esd", pick, tokens, preferred_element_type=jnp.float32
    ).astype(jnp.bfloat16)
    received = lax.all_to_all(outgoing, "expert", split_axis=0, concat_axis=0, tiled=True)

    large = slot_bound - slot_bound // 9
    answered, returned_small = expert_blocks(received, w_gate[0], w_up[0], w_down[0], large, 4)
    returned_large = lax.all_to_all(answered, "expert", split_axis=0, concat_axis=0, tiled=True)
    weight_parts = split_bf16(gate_values)
    experts = jnp.arange(experts_all, dtype=jnp.int32)
    slots = slot_of
    summed = None
    for begin, end, returned in ((large, slot_bound, returned_small), (0, large, returned_large)):
        stacked = jnp.stack(
            [
                jnp.sum(
                    jnp.where(
                        (expert_ids[:, :, None, None] == experts[None, None, :, None])
                        & (slots[:, :, None, None] == jnp.arange(begin, end)[None, None, None, :]),
                        part.astype(jnp.float32)[:, :, None, None],
                        0.0,
                    ),
                    axis=1,
                )
                for part in weight_parts
            ]
        ).astype(jnp.bfloat16)
        terms = jnp.einsum("ptes,esd->ptd", stacked, returned, preferred_element_type=jnp.float32)
        term = jnp.sum(terms, axis=0)
        summed = term if summed is None else summed + term
    return summed.astype(jnp.bfloat16)


def solution(mesh):
    placed = (
        P(("dp", "expert"), None),
        P(("dp", "expert"), None),
        P(("dp", "expert"), None),
        P("expert", None, None),
        P("expert", None, None),
        P("expert", None, None),
    )
    return jax.shard_map(
        shards, mesh=mesh, in_specs=placed, out_specs=P(("dp", "expert"), None), check_vma=False
    )
```
